128 devices in a mesh: row: 8 (over y, core), col: 16 (over z, x).
Axes of the slice: x: 4, y: 4, z: 4, core: 2. Of those that a mesh axis runs over, the one named last changes fastest.
Arguments:
- b_three: bfloat16 [256, 384, 1536], P(('row', 'col')), may hold values from -0.47851562 to 0.47851562
- e_occ: float32 [256], replicated, may hold values from -1.5 to -0.3
- e_vir: float32 [384], replicated, may hold values from 0.2 to 3
- c_occ: bfloat16 [768, 256], replicated, may hold values from -0.375 to 0.375
- pair_list: int32 [128, 16, 2], P(('row', 'col')), may hold values from 0 to 255, as said below
- pair_live: int32 [128, 16], P(('row', 'col')), may hold values from 0 to 1, as said below
Outputs:
- gamma_ao: bfloat16 [384, 1536, 768], P('row', 'col')
The draws below stay inside these ranges and needn't reach their ends.
Inputs may be any that keep to these rules, and one draw needn't show every extreme that they name: pair_list[w, p, 0] is one of the orbitals 2 w to 2 w + 1; pair_list[w, p, 1] is one of the orbitals 2 q to 2 q + 1 with q = (w // 16) * 16 + p. `pair_live`: every worker lists between 1 and 16 pairs; some worker lists all 16.
All inputs are finite; a program needn't handle non-finite values.
Results may differ from the reference program's by a relative error of at most 0.0053.
Values may be sent and summed in bfloat16 or wider, within the bound.
No kernel may reach another device: no remote copies, remote signals or barrier semaphores. Data moves between devices by JAX's collectives and lax.ppermute only.
A program may use at most 128 MiB of HBM per device.

```python
import jax
import jax.numpy as jnp
from jax import lax

V = 384
X = 1536
NBF = 768
ORB_DEV = 2
WORKERS = 128
PEERS = 16
O = 256


def draw_pair_list(key, part):
    worker_ids = jnp.arange(WORKERS, dtype=jnp.int32)[:, None]
    peer_ids = jnp.arange(PEERS, dtype=jnp.int32)[None, :]
    first_pick = jax.random.randint(jax.random.fold_in(key, 11), (WORKERS, PEERS), 0, ORB_DEV)
    second_pick = jax.random.randint(jax.random.fold_in(key, 12), (WORKERS, PEERS), 0, ORB_DEV)
    first = ORB_DEV * worker_ids + first_pick
    owner = worker_ids // PEERS * PEERS + peer_ids
    second = ORB_DEV * owner + second_pick
    return jnp.stack([first, second], -1).astype(jnp.int32)


def draw_pair_live(key, part):
    counts = jax.random.randint(jax.random.fold_in(key, 21), (WORKERS,), 1, PEERS + 1)
    busiest = jax.random.randint(jax.random.fold_in(key, 22), (), 0, WORKERS)
    counts = jnp.where(jnp.arange(WORKERS) == busiest, PEERS, counts)
    subkeys = jax.random.split(jax.random.fold_in(key, 23), WORKERS)
    ranks = jax.vmap(lambda subkey: jax.random.permutation(subkey, PEERS))(subkeys)
    return (ranks < counts[:, None]).astype(jnp.int32)


def block_levels(own_key, shape, shards, low, top_value):
    def one(dim, blocks):
        draws = jax.random.uniform(jax.random.fold_in(jax.random.fold_in(own_key, 6), dim), (blocks,), jnp.float32, low / len(shards), top_value / len(shards))
        return jnp.repeat(jnp.exp(draws), shape[dim] // blocks).reshape((-1,) + (1,) * (len(shape) - dim - 1))

    gain = one(*shards[0])
    for cut in shards[1:]:
        gain = gain * one(*cut)
    return gain


def noise(key, extent, width, reach, cuts=(), held_as=jnp.bfloat16):
    gain = block_levels(key, extent, cuts, -0.22, 0.18) if cuts else 1.0
    values = jax.random.normal(key, extent, jnp.float32) * width * gain
    return jnp.minimum(jnp.maximum(values, -reach), reach).astype(held_as)


def setup_inputs(seed: int = 0) -> dict:
    splits = jax.random.split(jax.random.key(seed), 7)
    return {
        "b_three": noise(splits[0], (O, V, X), 0.08, 0.47851562, ((0, 128),)),
        "e_occ": jnp.clip(jax.random.uniform(splits[1], (O,), jnp.float32, -1.5, -0.3), -1.5, -0.3),
        "e_vir": jnp.clip(jax.random.uniform(splits[2], (V,), jnp.float32, 0.2, 3.0), 0.2, 3.0),
        "c_occ": noise(splits[3], (NBF, O), O ** -0.5, 0.375),
        "pair_list": draw_pair_list(jax.random.fold_in(splits[6], 71), 0),
        "pair_live": draw_pair_live(jax.random.fold_in(splits[6], 71), 0),
    }


def reference(b_three, e_occ, e_vir, c_occ, pair_list, pair_live):
    flat_pairs = pair_list.reshape(-1, 2)
    flat_live = pair_live.reshape(-1)
    gamma = jnp.zeros(b_three.shape, jnp.float32)

    def advance(index, gamma):
        first_orb = flat_pairs[index, 0].astype(jnp.int32)
        second_orb = flat_pairs[index, 1].astype(jnp.int32)

        def accumulate(gamma):
            left_slab = lax.dynamic_index_in_dim(b_three, first_orb, 0, keepdims=False)
            right_slab = lax.dynamic_index_in_dim(b_three, second_orb, 0, keepdims=False)
            integrals = lax.dot_general(left_slab, right_slab, (((1,), (1,)), ((), ())), preferred_element_type=jnp.float32)
            denominator = (e_occ[first_orb] + e_occ[second_orb]) - e_vir[:, None] - e_vir[None, :]
            amplitude = integrals / denominator
            weighted = (2.0 * amplitude - amplitude.T).astype(jnp.bfloat16)
            addition = jnp.dot(weighted, right_slab, preferred_element_type=jnp.float32)
            current = lax.dynamic_index_in_dim(gamma, first_orb, 0, keepdims=False)
            return lax.dynamic_update_index_in_dim(gamma, current + addition, first_orb, 0)

        return lax.cond(flat_live[index] > 0, accumulate, lambda kept: kept, gamma)

    gamma = lax.fori_loop(0, flat_pairs.shape[0], advance, gamma)
    moved = gamma.astype(jnp.bfloat16).reshape(gamma.shape[0], -1)
    result = lax.dot_general(moved, c_occ, (((0,), (1,)), ((), ())), preferred_element_type=jnp.float32).astype(jnp.bfloat16)
    return result.reshape(b_three.shape[1], b_three.shape[2], c_occ.shape[0])
```

```python
import functools

import jax
import jax.numpy as jnp
from jax import lax
from jax.experimental import pallas as pl
from jax.experimental.pallas import tpu as pltpu
from jax.sharding import PartitionSpec as P


AXES = ("row", "col")
SIDE = 4


def shifted(kind, step):
    pairs = []
    for row in range(8):
        for z in range(SIDE):
            for x in range(SIDE):
                along_x = (row % 2 == 0) == (kind == "left")
                to_z, to_x = (z, (x + step) % SIDE) if along_x else ((z + step) % SIDE, x)
                pairs.append((row * 16 + z * SIDE + x, row * 16 + to_z * SIDE + to_x))
    return pairs


def send(value, kind, step):
    return lax.ppermute(value, AXES, shifted(kind, step))


def pair_body(table, place, energies, *refs, left_count):
    lefts = refs[:left_count]
    own, low, high, far_a, far_b, vir_row, vir_col, out_a, out_b = refs[left_count : left_count + 9]
    left_buf, right_buf, gamma, left_sem, right_sem = refs[left_count + 9 :]
    rights = (own, low, high, (far_a, far_b))
    worker = place[4]
    base = place[5]

    def right_of(n):
        return place[n]

    def entry(n):
        at = worker * 48 + right_of(n) * 2
        first = table[at]
        second = table[at + 1]
        return first, second, table[worker * 48 + 32 + right_of(n)]

    if left_count == 1:
        left_copies = [pltpu.make_async_copy(lefts[0], left_buf, left_sem.at[0])]
    else:
        left_copies = [
            pltpu.make_async_copy(lefts[s], left_buf.at[s], left_sem.at[s]) for s in range(2)
        ]
    for copy in left_copies:
        copy.start()
    for n in range(4):
        _, second, live = entry(n)
        slot = second % 2
        source = rights[n]
        if isinstance(source, tuple):
            for s in range(2):

                @pl.when((live > 0) & (slot == s))
                def _():
                    pltpu.make_async_copy(source[s], right_buf.at[n], right_sem.at[n]).start()
        else:

            @pl.when(live > 0)
            def _():
                pltpu.make_async_copy(source.at[slot], right_buf.at[n], right_sem.at[n]).start()

    gamma[...] = jnp.zeros_like(gamma)
    for copy in left_copies:
        copy.wait()

    def step(n, carry):
        first, second, live = entry(n)

        @pl.when(live > 0)
        def _():
            pltpu.make_async_copy(far_a, right_buf.at[n], right_sem.at[n]).wait()
            slot = first % 2
            right = right_buf[n]
            integrals = lax.dot_general(
                left_buf[slot], right, (((1,), (1,)), ((), ())), preferred_element_type=jnp.float32
            )
            denominator = energies[first] + energies[second] - vir_col[...] - vir_row[...]
            weighted = ((2.0 * integrals - integrals.T) / denominator).astype(jnp.bfloat16)
            gamma[slot] += jnp.dot(weighted, right, preferred_element_type=jnp.float32)

        return carry

    lax.fori_loop(0, 4, step, 0)
    out_a[...] = gamma[0].astype(out_a.dtype)
    out_b[...] = gamma[1].astype(out_b.dtype)


def partial_gamma(table, place, energies, lefts, rights, vir_row, vir_col, out_dtype):
    virt, aux = rights[0].shape[1:]
    slab = jax.ShapeDtypeStruct((virt, aux), out_dtype)
    anywhere = pl.BlockSpec(memory_space=pl.ANY)
    smem = pl.BlockSpec(memory_space=pltpu.SMEM)
    vmem = pl.BlockSpec(memory_space=pltpu.VMEM)
    return pl.pallas_call(
        functools.partial(pair_body, left_count=len(lefts)),
        out_shape=(slab, slab),
        in_specs=[smem, smem, smem] + [anywhere] * (len(lefts) + 5) + [vmem, vmem],
        out_specs=(vmem, vmem),
        scratch_shapes=[
            pltpu.VMEM((2, virt, aux), jnp.bfloat16),
            pltpu.VMEM((4, virt, aux), jnp.bfloat16),
            pltpu.VMEM((2, virt, aux), jnp.float32),
            pltpu.SemaphoreType.DMA((2,)),
            pltpu.SemaphoreType.DMA((4,)),
        ],
        compiler_params=pltpu.CompilerParams(vmem_limit_bytes=40 << 20),
    )(table, place, energies, *lefts, *rights, vir_row, vir_col)


def after(value, *others):
    return lax.optimization_barrier((value,) + others)[0]


def add(first, *others):
    total = first.astype(jnp.float32)
    for other in others:
        total = total + other.astype(jnp.float32)
    return total.astype(jnp.bfloat16)


def local(b_three, e_occ, e_vir, c_occ, pair_list, pair_live):
    own_count, virt_count, aux_count = b_three.shape
    peer_count = lax.axis_size("col")
    row_count = lax.axis_size("row")
    row = lax.axis_index("row")
    col = lax.axis_index("col")
    z, x = col // SIDE, col % SIDE
    even = row % 2 == 0

    def worker_at(kind, step):
        along_x = even if kind == "left" else ~even
        return jnp.where(
            along_x, z * SIDE + (x + step) % SIDE, (z + step) % SIDE * SIDE + x
        ).astype(jnp.int32)

    right_low = send(b_three, "right", 1)
    right_high = send(b_three, "right", -1)
    right_far_a = send(right_low[0], "right", 1)
    right_far_b = send(right_high[1], "right", -1)
    own = after(b_three, right_low, right_high)
    left_low = send(own, "left", 1)
    left_high = send(own, "left", -1)
    left_far_a = send(left_low[0], "left", 1)
    left_far_b = send(left_high[1], "left", -1)

    info = jnp.concatenate([pair_list.reshape(1, 32), pair_live.reshape(1, 16)], 1)
    table = lax.all_to_all(
        jnp.broadcast_to(info, (16, 48)), "col", split_axis=0, concat_axis=0, tiled=True
    ).reshape(768)
    rights = (b_three, right_low, right_high, right_far_a, right_far_b)
    right_places = [worker_at("right", step) for step in (0, -1, 1, 2)]
    vir_row, vir_col = e_vir.reshape(1, virt_count), e_vir.reshape(virt_count, 1)

    def partial(step, lefts, dtype=jnp.bfloat16):
        place = jnp.stack(right_places + [worker_at("left", step), row])
        return partial_gamma(table, place, e_occ, lefts, rights, vir_row, vir_col, dtype)

    own_a, own_b = partial(0, (b_three,), jnp.float32)
    low_a, low_b = partial(-1, (left_low,))
    high_a, high_b = partial(1, (left_high,))
    far_a, far_b = partial(2, (left_far_a, left_far_b))

    up_b = send(high_b, "left", 1)
    down_a = send(low_a, "left", -1)
    relay_a = send(far_a, "left", 1)
    relay_b = send(far_b, "left", -1)
    up_a = send(add(high_a, relay_a), "left", 1)
    down_b = send(add(low_b, relay_b), "left", -1)
    gamma_mo = jnp.stack([add(own_a, up_a, down_a), add(own_b, up_b, down_b)])

    virt_local = virt_count // row_count
    aux_local = aux_count // peer_count
    total_orbs = c_occ.shape[1]
    blocks = gamma_mo.reshape(own_count, row_count, virt_local, peer_count, aux_local)
    blocks = jnp.transpose(blocks, (1, 3, 0, 2, 4)).reshape(
        row_count * peer_count, own_count, virt_local * aux_local
    )
    regrouped = lax.all_to_all(blocks, AXES, split_axis=0, concat_axis=0, tiled=True)
    moved = regrouped.reshape(total_orbs, virt_local * aux_local)
    result = lax.dot_general(
        moved, c_occ, (((0,), (1,)), ((), ())), preferred_element_type=jnp.float32
    ).astype(jnp.bfloat16)
    return result.reshape(virt_local, aux_local, c_occ.shape[0])


def solution(mesh):
    return jax.shard_map(
        local,
        mesh=mesh,
        in_specs=(
            P(AXES, None, None),
            P(),
            P(),
            P(),
            P(AXES, None, None),
            P(AXES, None),
        ),
        out_specs=P("row", "col", None),
        check_vma=False,
    )
```

```python
import functools

import jax
import jax.numpy as jnp
import numpy as np
from jax import lax
from jax.experimental import pallas as pl
from jax.experimental.pallas import tpu as pltpu
from jax.sharding import PartitionSpec as P


AXES = ("row", "col")
SIDE = 4


def shifted(kind, step):
    pairs = []
    for row in range(8):
        for z in range(SIDE):
            for x in range(SIDE):
                along_x = (row % 2 == 0) == (kind == "left")
                to_z, to_x = (z, (x + step) % SIDE) if along_x else ((z + step) % SIDE, x)
                pairs.append((row * 16 + z * SIDE + x, row * 16 + to_z * SIDE + to_x))
    return pairs


def send(value, kind, step):
    return lax.ppermute(value, AXES, shifted(kind, step))


def pair_body(table, place, energies, left_a, left_b, *refs, slots):
    rights = refs[:8]
    vir_row, vir_col, out_a, out_b = refs[8:12]
    left_buf, right_buf, gamma, left_sem, right_sem = refs[12:]
    outs = (out_a, out_b)

    def entry(m):
        worker, right = place[4 + m // 4], place[m % 4]
        first = table[worker * 48 + right * 2]
        second = table[worker * 48 + right * 2 + 1]
        live = table[worker * 48 + 32 + right]
        side = m // 4
        wanted = slots[0] * (1 - side) + slots[1] * side
        return first, second, (live > 0) & (first % 2 == wanted)

    left_copies = [
        pltpu.make_async_copy(left, left_buf.at[s], left_sem.at[s])
        for s, left in enumerate((left_a, left_b))
    ]
    for copy in left_copies:
        copy.start()
    for m in range(8):
        _, second, taken = entry(m)
        for s in range(2):

            @pl.when(taken & (second % 2 == s))
            def _():
                pltpu.make_async_copy(
                    rights[2 * (m % 4) + s], right_buf.at[m], right_sem.at[m]
                ).start()

    gamma[...] = jnp.zeros_like(gamma)
    for copy in left_copies:
        copy.wait()

    def step(m, carry):
        first, second, taken = entry(m)

        @pl.when(taken)
        def _():
            pltpu.make_async_copy(rights[0], right_buf.at[m], right_sem.at[m]).wait()
            right = right_buf[m]
            integrals = lax.dot_general(
                left_buf[m // 4], right, (((1,), (1,)), ((), ())),
                preferred_element_type=jnp.float32,
            )
            denominator = energies[first] + energies[second] - vir_col[...] - vir_row[...]
            weighted = ((2.0 * integrals - integrals.T) / denominator).astype(jnp.bfloat16)
            gamma[m // 4] += jnp.dot(weighted, right, preferred_element_type=jnp.float32)

        return carry

    lax.fori_loop(0, 8, step, 0)
    for s in range(2):
        outs[s][...] = gamma[s].astype(outs[s].dtype)


def partial_gamma(table, place, energies, lefts, slots, rights, vir_row, vir_col, out_dtype, name):
    virt, aux = lefts[0].shape
    slab = jax.ShapeDtypeStruct((virt, aux), out_dtype)
    hbm = pl.BlockSpec(memory_space=pltpu.HBM)
    smem = pl.BlockSpec(memory_space=pltpu.SMEM)
    vmem = pl.BlockSpec(memory_space=pltpu.VMEM)
    return pl.pallas_call(
        functools.partial(pair_body, slots=slots),
        out_shape=(slab, slab),
        in_specs=[smem, smem, smem] + [hbm] * 10 + [vmem, vmem],
        out_specs=(vmem, vmem),
        scratch_shapes=[
            pltpu.VMEM((2, virt, aux), jnp.bfloat16),
            pltpu.VMEM((8, virt, aux), jnp.bfloat16),
            pltpu.VMEM((2, virt, aux), jnp.float32),
            pltpu.SemaphoreType.DMA((2,)),
            pltpu.SemaphoreType.DMA((8,)),
        ],
        compiler_params=pltpu.CompilerParams(vmem_limit_bytes=40 << 20),
        name=name,
    )(table, place, energies, *lefts, *rights, vir_row, vir_col)


def pack_body(own_a, own_b, up_a, down_a, up_b, down_b, out):
    c = pl.program_id(0)

    def emit(offset):
        for slot, parts in enumerate(((own_a, up_a, down_a), (own_b, up_b, down_b))):
            lanes = [p[:, offset : offset + 96].astype(jnp.float32) for p in parts]
            total = (lanes[0] + lanes[1] + lanes[2]).reshape(8, 2, 24, 96).astype(out.dtype)
            for half in range(2):
                q = 2 * slot + half
                out[:, 0, :, q * 96 : (q + 1) * 96] = total[:, half]

    for k in range(4):

        @pl.when(c % 4 == k)
        def _():
            emit(k * 96)


def pack(own_a, own_b, up_a, down_a, up_b, down_b):
    wide = pl.BlockSpec((384, 384), lambda c: (0, c // 4))
    return pl.pallas_call(
        pack_body,
        grid=(16,),
        out_shape=jax.ShapeDtypeStruct((8, 16, 24, 384), jnp.bfloat16),
        in_specs=[wide] * 6,
        out_specs=pl.BlockSpec((8, 1, 24, 384), lambda c: (0, c, 0, 0)),
        name="pack",
    )(own_a, own_b, up_a, down_a, up_b, down_b)


def finish_body(blocks, coeff, out, wide):
    step = pl.program_id(0)

    @pl.when(step == 0)
    def _():
        def spread(w, carry):
            for q in range(4):
                rows = pl.ds((2 * w + q // 2) * 48 + (q % 2) * 24, 24)
                wide[rows, 0:96] = blocks[w, :, q * 96 : (q + 1) * 96].astype(jnp.float32)
            return carry

        lax.fori_loop(0, 128, spread, 0, unroll=4)

    for k in range(out.shape[0]):
        rows = wide[pl.ds(step * out.shape[0] + k, 256, stride=48), :].astype(jnp.bfloat16)
        result = lax.dot_general(
            rows, coeff[...], (((0,), (1,)), ((), ())), preferred_element_type=jnp.float32
        )
        out[k] = result[0:96].astype(out.dtype)


def finish(blocks, coeff):
    rows = 6
    return pl.pallas_call(
        finish_body,
        grid=(48 // rows,),
        out_shape=jax.ShapeDtypeStruct((48, 96, 768), jnp.bfloat16),
        in_specs=[
            pl.BlockSpec((128, 24, 384), lambda s: (0, 0, 0)),
            pl.BlockSpec((768, 256), lambda s: (0, 0)),
        ],
        out_specs=pl.BlockSpec((rows, 96, 768), lambda s: (s, 0, 0)),
        scratch_shapes=[pltpu.VMEM((256 * 48, 128), jnp.float32)],
        name="finish",
    )(blocks, coeff)


def after(value, *others):
    return lax.optimization_barrier((value,) + others)[0]


def add(first, *others):
    total = first.astype(jnp.float32)
    for other in others:
        total = total + other.astype(jnp.float32)
    return total.astype(jnp.bfloat16)


def places():
    rows = []
    for row in range(8):
        for z in range(SIDE):
            for x in range(SIDE):
                along_x = [z * SIDE + (x + d) % SIDE for d in (0, -1, 1, 2)]
                along_z = [(z + d) % SIDE * SIDE + x for d in (0, -1, 1, 2)]
                rows.append(along_z + along_x if row % 2 == 0 else along_x + along_z)
    return np.array(rows, np.int32)


def local(b_three, e_occ, e_vir, c_occ, pair_list, pair_live):
    own_count, virt_count, aux_count = b_three.shape
    device = lax.axis_index("row") * 16 + lax.axis_index("col")
    own = (b_three[0], b_three[1])

    right_low_a, right_low_b = send(own[0], "right", 1), send(own[1], "right", 1)
    right_high_a, right_high_b = send(own[0], "right", -1), send(own[1], "right", -1)

    info = jnp.concatenate([pair_list.reshape(1, 32), pair_live.reshape(1, 16)], 1)
    table = lax.all_to_all(
        jnp.broadcast_to(info, (16, 48)), "col", split_axis=0, concat_axis=0, tiled=True
    ).reshape(768)

    own_a, own_b, _, _ = lax.optimization_barrier((own[0], own[1], right_low_a, table))
    left_low_a = send(own_a, "left", 1)
    left_high_b = send(own_b, "left", -1)
    right_far_a = send(right_low_a, "right", 1)
    right_far_b = send(right_high_b, "right", -1)
    own_a, own_b, _, _ = lax.optimization_barrier((own_a, own_b, left_low_a, right_far_a))
    left_far_a = send(left_low_a, "left", 1)
    left_far_b = send(left_high_b, "left", -1)
    left_low_b = send(own_b, "left", 1)
    left_high_a = send(own_a, "left", -1)

    rights = (*own, right_low_a, right_low_b, right_high_a, right_high_b, right_far_a, right_far_b)
    vir_row, vir_col = e_vir.reshape(1, virt_count), e_vir.reshape(virt_count, 1)
    place = lax.dynamic_index_in_dim(jnp.asarray(places()), device, 0, keepdims=False)

    def partial(name, lefts, which, slots, dtype=jnp.bfloat16):
        here = jnp.concatenate([place[:4]] + [place[4 + k : 5 + k] for k in which])
        return partial_gamma(table, here, e_occ, lefts, slots, rights, vir_row, vir_col, dtype, name)

    sum_a, sum_b = partial("own", own, (0, 0), (0, 1), jnp.float32)
    low_a, high_b = partial("near", (left_low_a, left_high_b), (1, 2), (0, 1))
    far_a, far_b = partial("far", (left_far_a, left_far_b), (3, 3), (0, 1))
    low_b, high_a = partial("late", (left_low_b, left_high_a), (1, 2), (1, 0))

    up_b = send(high_b, "left", 1)
    down_a = send(low_a, "left", -1)
    relay_a = send(far_a, "left", 1)
    relay_b = send(far_b, "left", -1)
    up_a = send(add(high_a, relay_a), "left", 1)
    down_b = send(add(low_b, relay_b), "left", -1)

    blocks = pack(sum_a, sum_b, up_a, down_a, up_b, down_b).reshape(128, 24, 384)
    moved = lax.all_to_all(blocks, AXES, split_axis=0, concat_axis=0, tiled=True)
    return finish(moved, c_occ)


def solution(mesh):
    return jax.shard_map(
        local,
        mesh=mesh,
        in_specs=(
            P(AXES, None, None),
            P(),
            P(),
            P(),
            P(AXES, None, None),
            P(AXES, None),
        ),
        out_specs=P("row", "col", None),
        check_vma=False,
    )
```

```python
import functools

import jax
import jax.numpy as jnp
import numpy as np
from jax import lax
from jax.experimental import pallas as pl
from jax.experimental.pallas import tpu as pltpu
from jax.sharding import PartitionSpec as P


AXES = ("row", "col")
SIDE = 4


def shifted(kind, step):
    pairs = []
    for row in range(8):
        for z in range(SIDE):
            for x in range(SIDE):
                along_x = (row % 2 == 0) == (kind == "left")
                to_z, to_x = (z, (x + step) % SIDE) if along_x else ((z + step) % SIDE, x)
                pairs.append((row * 16 + z * SIDE + x, row * 16 + to_z * SIDE + to_x))
    return pairs


def send(value, kind, step):
    return lax.ppermute(value, AXES, shifted(kind, step))


def pair_body(table, place, energies, left_a, left_b, *refs, slots):
    rights = refs[:8]
    vir_row, vir_col, out_a, out_b = refs[8:12]
    left_buf, right_buf, gamma, left_sem, right_sem = refs[12:]
    outs = (out_a, out_b)

    def entry(m):
        worker, right = place[4 + m // 4], place[m % 4]
        first = table[worker * 48 + right * 2]
        second = table[worker * 48 + right * 2 + 1]
        live = table[worker * 48 + 32 + right]
        side = m // 4
        wanted = slots[0] * (1 - side) + slots[1] * side
        return first, second, (live > 0) & (first % 2 == wanted)

    left_copies = [
        pltpu.make_async_copy(left, left_buf.at[s], left_sem.at[s])
        for s, left in enumerate((left_a, left_b))
    ]
    for copy in left_copies:
        copy.start()
    for m in range(8):
        _, second, taken = entry(m)
        for s in range(2):

            @pl.when(taken & (second % 2 == s))
            def _():
                pltpu.make_async_copy(
                    rights[2 * (m % 4) + s], right_buf.at[m], right_sem.at[m]
                ).start()

    gamma[...] = jnp.zeros_like(gamma)
    for copy in left_copies:
        copy.wait()

    def step(m, carry):
        first, second, taken = entry(m)

        @pl.when(taken)
        def _():
            pltpu.make_async_copy(rights[0], right_buf.at[m], right_sem.at[m]).wait()
            right = right_buf[m]
            integrals = lax.dot_general(
                left_buf[m // 4], right, (((1,), (1,)), ((), ())),
                preferred_element_type=jnp.float32,
            )
            denominator = energies[first] + energies[second] - vir_col[...] - vir_row[...]
            weighted = ((2.0 * integrals - integrals.T) / denominator).astype(jnp.bfloat16)
            gamma[m // 4] += jnp.dot(weighted, right, preferred_element_type=jnp.float32)

        return carry

    lax.fori_loop(0, 8, step, 0)
    for s in range(2):
        outs[s][...] = gamma[s].astype(outs[s].dtype)


def partial_gamma(table, place, energies, lefts, slots, rights, vir_row, vir_col, out_dtype):
    virt, aux = lefts[0].shape
    slab = jax.ShapeDtypeStruct((virt, aux), out_dtype)
    hbm = pl.BlockSpec(memory_space=pltpu.HBM)
    smem = pl.BlockSpec(memory_space=pltpu.SMEM)
    vmem = pl.BlockSpec(memory_space=pltpu.VMEM)
    return pl.pallas_call(
        functools.partial(pair_body, slots=slots),
        out_shape=(slab, slab),
        in_specs=[smem, smem, smem] + [hbm] * 10 + [vmem, vmem],
        out_specs=(vmem, vmem),
        scratch_shapes=[
            pltpu.VMEM((2, virt, aux), jnp.bfloat16),
            pltpu.VMEM((8, virt, aux), jnp.bfloat16),
            pltpu.VMEM((2, virt, aux), jnp.float32),
            pltpu.SemaphoreType.DMA((2,)),
            pltpu.SemaphoreType.DMA((8,)),
        ],
        compiler_params=pltpu.CompilerParams(vmem_limit_bytes=40 << 20),
    )(table, place, energies, *lefts, *rights, vir_row, vir_col)


def pack_body(own_a, own_b, up_a, down_a, up_b, down_b, out, total, block):
    for slot, parts in enumerate(((own_a, up_a, down_a), (own_b, up_b, down_b))):
        for k in range(12):
            lanes = slice(k * 128, (k + 1) * 128)
            own, up, down = (part[:, lanes].astype(jnp.float32) for part in parts)
            total[slot * 12 + k] = own + up + down
    for c in range(16):
        tile, offset = divmod(c * 96, 128)
        for slot in range(2):
            pieces = []
            for q in range(4):
                rows = pl.ds(q, 96, stride=4)
                piece = total[slot * 12 + tile, rows, :]
                if offset > 32:
                    piece = jnp.concatenate([piece, total[slot * 12 + tile + 1, rows, :]], 1)
                pieces.append(piece[:, offset : offset + 96])
            value = jnp.concatenate(pieces, 1)
            for k in range(3):
                block[c % 2 * 3 + k, pl.ds(slot, 96, stride=2), :] = value[:, k * 128 : (k + 1) * 128]
        for r in range(8):
            for k in range(3):
                out[r * 16 + c, :, k * 128 : (k + 1) * 128] = block[
                    c % 2 * 3 + k, r * 24 : (r + 1) * 24
                ].astype(out.dtype)


def pack(own_a, own_b, up_a, down_a, up_b, down_b):
    vmem = pl.BlockSpec(memory_space=pltpu.VMEM)
    return pl.pallas_call(
        pack_body,
        out_shape=jax.ShapeDtypeStruct((128, 24, 384), jnp.bfloat16),
        in_specs=[vmem] * 6,
        out_specs=vmem,
        scratch_shapes=[
            pltpu.VMEM((24, 384, 128), jnp.float32),
            pltpu.VMEM((6, 192, 128), jnp.float32),
        ],
        compiler_params=pltpu.CompilerParams(vmem_limit_bytes=32 << 20),
        name="pack",
    )(own_a, own_b, up_a, down_a, up_b, down_b)


def finish_body(blocks, coeff, out, wide):
    step = pl.program_id(0)

    @pl.when(step == 0)
    def _():
        for k in range(3):
            wide[k] = blocks[:, k * 128 : (k + 1) * 128].astype(jnp.float32)

    per_step = out.shape[0] // 4
    for k in range(per_step):
        t = step * per_step + k
        rows = jnp.concatenate(
            [
                jnp.concatenate([wide[k, pl.ds(2 * t + s, 128, stride=24), :] for k in range(3)], 1)
                for s in range(2)
            ],
            0,
        ).astype(jnp.bfloat16)
        result = lax.dot_general(
            rows, coeff[...], (((0,), (1,)), ((), ())),
            preferred_element_type=jnp.float32,
        )
        out[4 * k : 4 * k + 4] = result.reshape(4, 96, 768).astype(out.dtype)


def finish(blocks, coeff):
    rows = 12
    return pl.pallas_call(
        finish_body,
        grid=(48 // rows,),
        out_shape=jax.ShapeDtypeStruct((48, 96, 768), jnp.bfloat16),
        in_specs=[
            pl.BlockSpec((128 * 24, 384), lambda s: (0, 0)),
            pl.BlockSpec((768, 256), lambda s: (0, 0)),
        ],
        out_specs=pl.BlockSpec((rows, 96, 768), lambda s: (s, 0, 0)),
        scratch_shapes=[pltpu.VMEM((3, 128 * 24, 128), jnp.float32)],
        compiler_params=pltpu.CompilerParams(vmem_limit_bytes=32 << 20),
        name="finish",
    )(blocks, coeff)


def add(first, *others):
    total = first.astype(jnp.float32)
    for other in others:
        total = total + other.astype(jnp.float32)
    return total.astype(jnp.bfloat16)


def places():
    rows = []
    for row in range(8):
        for z in range(SIDE):
            for x in range(SIDE):
                along_x = [z * SIDE + (x + d) % SIDE for d in (0, -1, 1, 2)]
                along_z = [(z + d) % SIDE * SIDE + x for d in (0, -1, 1, 2)]
                rows.append(along_z + along_x if row % 2 == 0 else along_x + along_z)
    return np.array(rows, np.int32)


def local(b_three, e_occ, e_vir, c_occ, pair_list, pair_live):
    _, virt_count, _ = b_three.shape
    device = lax.axis_index("row") * 16 + lax.axis_index("col")
    own = (b_three[0], b_three[1])

    right_low_a, right_low_b = send(own[0], "right", 1), send(own[1], "right", 1)
    right_high_a, right_high_b = send(own[0], "right", -1), send(own[1], "right", -1)

    info = jnp.concatenate([pair_list.reshape(1, 32), pair_live.reshape(1, 16)], 1)
    table = lax.all_to_all(
        jnp.broadcast_to(info, (16, 48)), "col", split_axis=0, concat_axis=0, tiled=True
    ).reshape(768)

    wave = lax.optimization_barrier(
        (*own, right_low_a, right_low_b, right_high_a, right_high_b, table)
    )
    own_a, own_b, right_low_a, right_low_b, right_high_a, right_high_b, table = wave
    left_low_a = send(own_a, "left", 1)
    left_high_b = send(own_b, "left", -1)
    right_far_a = send(right_low_a, "right", 1)
    right_far_b = send(right_high_b, "right", -1)
    wave = lax.optimization_barrier(
        (own_a, own_b, left_low_a, left_high_b, right_far_a, right_far_b)
    )
    own_a, own_b, left_low_a, left_high_b, right_far_a, right_far_b = wave
    left_far_a = send(left_low_a, "left", 1)
    left_far_b = send(left_high_b, "left", -1)
    left_low_b = send(own_b, "left", 1)
    left_high_a = send(own_a, "left", -1)

    rights = (*own, right_low_a, right_low_b, right_high_a, right_high_b, right_far_a, right_far_b)
    vir_row, vir_col = e_vir.reshape(1, virt_count), e_vir.reshape(virt_count, 1)
    place = lax.dynamic_index_in_dim(jnp.asarray(places()), device, 0, keepdims=False)

    def partial(lefts, which, slots, dtype=jnp.bfloat16):
        here = jnp.concatenate([place[:4]] + [place[4 + k : 5 + k] for k in which])
        return partial_gamma(table, here, e_occ, lefts, slots, rights, vir_row, vir_col, dtype)

    low_a, high_b = partial((left_low_a, left_high_b), (1, 2), (0, 1))
    sum_a, sum_b = partial(own, (0, 0), (0, 1), jnp.float32)
    low_a, high_b, _, _ = lax.optimization_barrier((low_a, high_b, left_far_a, left_far_b))
    up_b = send(high_b, "left", 1)
    down_a = send(low_a, "left", -1)
    far_a, far_b = partial((left_far_a, left_far_b), (3, 3), (0, 1))
    low_b, high_a = partial((left_low_b, left_high_a), (1, 2), (1, 0))

    relay_a = send(far_a, "left", 1)
    relay_b = send(far_b, "left", -1)
    up_a = send(add(high_a, relay_a), "left", 1)
    down_b = send(add(low_b, relay_b), "left", -1)

    blocks = pack(sum_a, sum_b, up_a, down_a, up_b, down_b)
    moved = lax.all_to_all(blocks, AXES, split_axis=0, concat_axis=0, tiled=True)
    coeff = c_occ.reshape(-1, 128, 2).transpose(0, 2, 1).reshape(-1, 256)
    return finish(moved.reshape(128 * 24, 384), coeff)


def solution(mesh):
    return jax.shard_map(
        local,
        mesh=mesh,
        in_specs=(
            P(AXES, None, None),
            P(),
            P(),
            P(),
            P(AXES, None, None),
            P(AXES, None),
        ),
        out_specs=P("row", "col", None),
        check_vma=False,
    )
```

```python
import functools

import jax
import jax.numpy as jnp
import numpy as np
from jax import lax
from jax.experimental import pallas as pl
from jax.experimental.pallas import tpu as pltpu
from jax.sharding import PartitionSpec as P


AXES = ("row", "col")
SIDE = 4


def shifted(kind, step):
    pairs = []
    for row in range(8):
        for z in range(SIDE):
            for x in range(SIDE):
                along_x = (row % 2 == 0) == (kind == "left")
                to_z, to_x = (z, (x + step) % SIDE) if along_x else ((z + step) % SIDE, x)
                pairs.append((row * 16 + z * SIDE + x, row * 16 + to_z * SIDE + to_x))
    return pairs


def send(value, kind, step):
    return lax.ppermute(value, AXES, shifted(kind, step))


def pair_body(place, table_a, table_b, energies, left_a, left_b, *refs, slots):
    rights = refs[:8]
    vir_row, vir_col, out_a, out_b = refs[8:12]
    left_buf, right_buf, gamma, left_sem, right_sem = refs[12:]
    outs = (out_a, out_b)

    def entry(m):
        side, right = m // 4, place[m % 4]
        at_a, at_b = (lambda k: table_a[0, k]), (lambda k: table_b[0, k])

        def pick(k):
            return jnp.where(side == 0, at_a(k), at_b(k))

        first, second, live = pick(right * 2), pick(right * 2 + 1), pick(32 + right)
        wanted = jnp.where(side == 0, slots[0], slots[1])
        return first, second, (live > 0) & (first % 2 == wanted)

    left_copies = [
        pltpu.make_async_copy(left, left_buf.at[s], left_sem.at[s])
        for s, left in enumerate((left_a, left_b))
    ]
    for copy in left_copies:
        copy.start()
    for m in range(8):
        _, second, taken = entry(m)
        for s in range(2):

            @pl.when(taken & (second % 2 == s))
            def _():
                pltpu.make_async_copy(
                    rights[2 * (m % 4) + s], right_buf.at[m], right_sem.at[m]
                ).start()

    gamma[...] = jnp.zeros_like(gamma)
    for copy in left_copies:
        copy.wait()

    def step(m, carry):
        first, second, taken = entry(m)

        @pl.when(taken)
        def _():
            pltpu.make_async_copy(rights[0], right_buf.at[m], right_sem.at[m]).wait()
            right = right_buf[m]
            integrals = lax.dot_general(
                left_buf[m // 4], right, (((1,), (1,)), ((), ())),
                preferred_element_type=jnp.float32,
            )
            denominator = energies[first] + energies[second] - vir_col[...] - vir_row[...]
            weighted = ((2.0 * integrals - integrals.T) / denominator).astype(jnp.bfloat16)
            gamma[m // 4] += jnp.dot(weighted, right, preferred_element_type=jnp.float32)

        return carry

    lax.fori_loop(0, 8, step, 0)
    for s in range(2):
        outs[s][...] = gamma[s].astype(outs[s].dtype)


def partial_gamma(place, tables, energies, lefts, slots, rights, vir_row, vir_col, out_dtype):
    virt, aux = lefts[0].shape
    slab = jax.ShapeDtypeStruct((virt, aux), out_dtype)
    hbm = pl.BlockSpec(memory_space=pltpu.HBM)
    smem = pl.BlockSpec(memory_space=pltpu.SMEM)
    vmem = pl.BlockSpec(memory_space=pltpu.VMEM)
    return pl.pallas_call(
        functools.partial(pair_body, slots=slots),
        out_shape=(slab, slab),
        in_specs=[smem, smem, smem, smem] + [hbm] * 10 + [vmem, vmem],
        out_specs=(vmem, vmem),
        scratch_shapes=[
            pltpu.VMEM((2, virt, aux), jnp.bfloat16),
            pltpu.VMEM((8, virt, aux), jnp.bfloat16),
            pltpu.VMEM((2, virt, aux), jnp.float32),
            pltpu.SemaphoreType.DMA((2,)),
            pltpu.SemaphoreType.DMA((8,)),
        ],
        compiler_params=pltpu.CompilerParams(vmem_limit_bytes=40 << 20),
    )(place, *tables, energies, *lefts, *rights, vir_row, vir_col)


def pack_body(own_a, own_b, up_a, down_a, up_b, down_b, out, total, block):
    for slot, parts in enumerate(((own_a, up_a, down_a), (own_b, up_b, down_b))):
        for k in range(12):
            lanes = slice(k * 128, (k + 1) * 128)
            own, up, down = (part[:, lanes].astype(jnp.float32) for part in parts)
            total[slot * 12 + k] = own + up + down
    for c in range(16):
        tile, offset = divmod(c * 96, 128)
        for slot in range(2):
            pieces = []
            for q in range(4):
                rows = pl.ds(q, 96, stride=4)
                piece = total[slot * 12 + tile, rows, :]
                if offset > 32:
                    piece = jnp.concatenate([piece, total[slot * 12 + tile + 1, rows, :]], 1)
                pieces.append(piece[:, offset : offset + 96])
            value = jnp.concatenate(pieces, 1)
            for k in range(3):
                block[c % 2 * 3 + k, pl.ds(slot, 96, stride=2), :] = value[:, k * 128 : (k + 1) * 128]
        for r in range(8):
            for k in range(3):
                out[r * 16 + c, :, k * 128 : (k + 1) * 128] = block[
                    c % 2 * 3 + k, r * 24 : (r + 1) * 24
                ].astype(out.dtype)


def pack(own_a, own_b, up_a, down_a, up_b, down_b):
    vmem = pl.BlockSpec(memory_space=pltpu.VMEM)
    return pl.pallas_call(
        pack_body,
        out_shape=jax.ShapeDtypeStruct((128, 24, 384), jnp.bfloat16),
        in_specs=[vmem] * 6,
        out_specs=vmem,
        scratch_shapes=[
            pltpu.VMEM((24, 384, 128), jnp.float32),
            pltpu.VMEM((6, 192, 128), jnp.float32),
        ],
        compiler_params=pltpu.CompilerParams(vmem_limit_bytes=32 << 20),
        name="pack",
    )(own_a, own_b, up_a, down_a, up_b, down_b)


def finish_body(blocks, coeff, out, wide):
    step = pl.program_id(0)

    @pl.when(step == 0)
    def _():
        for k in range(3):
            wide[k] = blocks[:, k * 128 : (k + 1) * 128].astype(jnp.float32)

    per_step = out.shape[0] // 4
    for k in range(per_step):
        t = step * per_step + k
        rows = jnp.concatenate(
            [
                jnp.concatenate([wide[k, pl.ds(2 * t + s, 128, stride=24), :] for k in range(3)], 1)
                for s in range(2)
            ],
            0,
        ).astype(jnp.bfloat16)
        result = lax.dot_general(
            rows, coeff[...], (((0,), (1,)), ((), ())),
            preferred_element_type=jnp.float32,
        )
        out[4 * k : 4 * k + 4] = result.reshape(4, 96, 768).astype(out.dtype)


def finish(blocks, coeff):
    rows = 12
    return pl.pallas_call(
        finish_body,
        grid=(48 // rows,),
        out_shape=jax.ShapeDtypeStruct((48, 96, 768), jnp.bfloat16),
        in_specs=[
            pl.BlockSpec((128 * 24, 384), lambda s: (0, 0)),
            pl.BlockSpec((768, 256), lambda s: (0, 0)),
        ],
        out_specs=pl.BlockSpec((rows, 96, 768), lambda s: (s, 0, 0)),
        scratch_shapes=[pltpu.VMEM((3, 128 * 24, 128), jnp.float32)],
        compiler_params=pltpu.CompilerParams(vmem_limit_bytes=32 << 20),
        name="finish",
    )(blocks, coeff)


def add(first, *others):
    total = first.astype(jnp.float32)
    for other in others:
        total = total + other.astype(jnp.float32)
    return total.astype(jnp.bfloat16)


def right_columns():
    rows = []
    for row in range(8):
        for z in range(SIDE):
            for x in range(SIDE):
                along_x = [z * SIDE + (x + d) % SIDE for d in (0, -1, 1, 2)]
                along_z = [(z + d) % SIDE * SIDE + x for d in (0, -1, 1, 2)]
                rows.append(along_z if row % 2 == 0 else along_x)
    return np.array(rows, np.int32).reshape(-1)


def local(b_three, e_occ, e_vir, c_occ, pair_list, pair_live):
    _, virt_count, _ = b_three.shape
    device = lax.axis_index("row") * 16 + lax.axis_index("col")
    own = (b_three[0], b_three[1])

    right_low_a, right_low_b = send(own[0], "right", 1), send(own[1], "right", 1)
    right_high_a, right_high_b = send(own[0], "right", -1), send(own[1], "right", -1)
    info = jnp.concatenate([pair_list.reshape(1, 32), pair_live.reshape(1, 16)], 1)

    tables = [info]
    for step in (1, -1, 2):
        tables.append(send(info, "left", step))
    wave = lax.optimization_barrier((*own, right_low_a, right_low_b, right_high_a, right_high_b))
    own_a, own_b, right_low_a, right_low_b, right_high_a, right_high_b = wave
    left_low_a = send(own_a, "left", 1)
    left_high_b = send(own_b, "left", -1)
    right_far_a = send(right_low_a, "right", 1)
    right_far_b = send(right_high_b, "right", -1)
    wave = lax.optimization_barrier(
        (own_a, own_b, left_low_a, left_high_b, right_far_a, right_far_b)
    )
    own_a, own_b, left_low_a, left_high_b, right_far_a, right_far_b = wave
    left_far_a = send(left_low_a, "left", 1)
    left_far_b = send(left_high_b, "left", -1)
    own_a, own_b, left_far_a, left_far_b = lax.optimization_barrier(
        (own_a, own_b, left_far_a, left_far_b)
    )
    left_low_b = send(own_b, "left", 1)
    left_high_a = send(own_a, "left", -1)

    rights = (*own, right_low_a, right_low_b, right_high_a, right_high_b, right_far_a, right_far_b)
    vir_row, vir_col = e_vir.reshape(1, virt_count), e_vir.reshape(virt_count, 1)
    place = lax.dynamic_slice_in_dim(jnp.asarray(right_columns()), device * 4, 4)

    def partial(lefts, which, slots, dtype=jnp.bfloat16):
        chosen = [tables[k] for k in which]
        return partial_gamma(place, chosen, e_occ, lefts, slots, rights, vir_row, vir_col, dtype)

    low_a, high_b = partial((left_low_a, left_high_b), (1, 2), (0, 1))
    up_b = send(high_b, "left", 1)
    down_a = send(low_a, "left", -1)
    sum_a, sum_b = partial(own, (0, 0), (0, 1), jnp.float32)
    far_a, far_b = partial((left_far_a, left_far_b), (3, 3), (0, 1))
    relay_a = send(far_a, "left", 1)
    relay_b = send(far_b, "left", -1)
    low_b, high_a = partial((left_low_b, left_high_a), (1, 2), (1, 0))
    up_a = send(add(high_a, relay_a), "left", 1)
    down_b = send(add(low_b, relay_b), "left", -1)

    blocks = pack(sum_a, sum_b, up_a, down_a, up_b, down_b)
    moved = lax.all_to_all(blocks, AXES, split_axis=0, concat_axis=0, tiled=True)
    coeff = c_occ.reshape(-1, 128, 2).transpose(0, 2, 1).reshape(-1, 256)
    return finish(moved.reshape(128 * 24, 384), coeff)


def solution(mesh):
    return jax.shard_map(
        local,
        mesh=mesh,
        in_specs=(
            P(AXES, None, None),
            P(),
            P(),
            P(),
            P(AXES, None, None),
            P(AXES, None),
        ),
        out_specs=P("row", "col", None),
        check_vma=False,
    )
```

```python
import functools

import jax
import jax.numpy as jnp
from jax import lax
from jax.experimental import pallas as pl
from jax.experimental.pallas import tpu as pltpu
from jax.sharding import PartitionSpec as P


AXES = ("row", "col")
SIDE = 4


def shifted(kind, step):
    pairs = []
    for row in range(8):
        for z in range(SIDE):
            for x in range(SIDE):
                along_x = (row % 2 == 0) == (kind == "left")
                to_z, to_x = (z, (x + step) % SIDE) if along_x else ((z + step) % SIDE, x)
                pairs.append((row * 16 + z * SIDE + x, row * 16 + to_z * SIDE + to_x))
    return pairs


def send(value, kind, step):
    return lax.ppermute(value, AXES, shifted(kind, step))


def pair_body(device, table_a, table_b, energies, own, *refs, slots):
    lefts, rights = refs[:2], refs[2:8]
    levels, out_a, out_b = refs[8:11]
    left_buf, right_buf, gamma, across, left_sem, right_sem = refs[11:]
    outs = (out_a, out_b)
    rights = (own.at[0], own.at[1], *rights)
    if lefts[0].shape == own.shape:
        lefts = (own.at[0], own.at[1])
    col = device[0] % 16
    z, x = col // SIDE, col % SIDE
    even = device[0] // 16 % 2 == 0
    columns = [
        jnp.where(even, (z + d) % SIDE * SIDE + x, z * SIDE + (x + d) % SIDE) for d in (0, 3, 1, 2)
    ]

    def entry(m):
        side, n = m // 4, m % 4
        right = jnp.where(
            n < 2, jnp.where(n == 0, columns[0], columns[1]), jnp.where(n == 2, columns[2], columns[3])
        )

        def pick(k):
            return jnp.where(side == 0, table_a[0, k], table_b[0, k])

        first, second, live = pick(right * 2), pick(right * 2 + 1), pick(32 + right)
        wanted = jnp.where(side == 0, slots[0], slots[1])
        return first, second, (live > 0) & (first % 2 == wanted)

    left_copies = [
        pltpu.make_async_copy(left, left_buf.at[s], left_sem.at[s]) for s, left in enumerate(lefts)
    ]
    for copy in left_copies:
        copy.start()
    for m in range(8):
        _, second, taken = entry(m)
        for s in range(2):

            @pl.when(taken & (second % 2 == s))
            def _():
                pltpu.make_async_copy(
                    rights[2 * (m % 4) + s], right_buf.at[m], right_sem.at[m]
                ).start()

    gamma[...] = jnp.zeros_like(gamma)
    row = levels[...].reshape(1, levels.shape[-1])
    across[...] = jnp.broadcast_to(row, across.shape).T
    for copy in left_copies:
        copy.wait()

    def step(m, carry):
        first, second, taken = entry(m)

        @pl.when(taken)
        def _():
            pltpu.make_async_copy(rights[0], right_buf.at[m], right_sem.at[m]).wait()
            right = right_buf[m]
            integrals = lax.dot_general(
                left_buf[m // 4], right, (((1,), (1,)), ((), ())),
                preferred_element_type=jnp.float32,
            )
            denominator = energies[first] + energies[second] - across[...] - row
            weighted = ((2.0 * integrals - integrals.T) / denominator).astype(jnp.bfloat16)
            gamma[m // 4] += jnp.dot(weighted, right, preferred_element_type=jnp.float32)

        return carry

    lax.fori_loop(0, 8, step, 0)
    for s in range(2):
        outs[s][...] = gamma[s].astype(outs[s].dtype)


def partial_gamma(device, tables, energies, own, lefts, slots, rights, levels, out_dtype):
    virt, aux = own.shape[1:]
    slab = jax.ShapeDtypeStruct((virt, aux), out_dtype)
    hbm = pl.BlockSpec(memory_space=pltpu.HBM)
    smem = pl.BlockSpec(memory_space=pltpu.SMEM)
    vmem = pl.BlockSpec(memory_space=pltpu.VMEM)
    return pl.pallas_call(
        functools.partial(pair_body, slots=slots),
        out_shape=(slab, slab),
        in_specs=[smem, smem, smem, smem] + [hbm] * 9 + [vmem],
        out_specs=(vmem, vmem),
        scratch_shapes=[
            pltpu.VMEM((2, virt, aux), jnp.bfloat16),
            pltpu.VMEM((8, virt, aux), jnp.bfloat16),
            pltpu.VMEM((2, virt, aux), jnp.float32),
            pltpu.VMEM((virt, virt), jnp.float32),
            pltpu.SemaphoreType.DMA((2,)),
            pltpu.SemaphoreType.DMA((8,)),
        ],
        compiler_params=pltpu.CompilerParams(vmem_limit_bytes=40 << 20),
    )(device, *tables, energies, own, *lefts, *rights, levels)


def pack_body(own_a, own_b, up_a, down_a, up_b, down_b, out, total, block):
    for slot, parts in enumerate(((own_a, up_a, down_a), (own_b, up_b, down_b))):
        for k in range(12):
            lanes = slice(k * 128, (k + 1) * 128)
            own, up, down = (part[:, lanes].astype(jnp.float32) for part in parts)
            total[slot * 12 + k] = own + up + down
    for c in range(16):
        tile, offset = divmod(c * 96, 128)
        for slot in range(2):
            pieces = []
            for q in range(4):
                rows = pl.ds(q, 96, stride=4)
                piece = total[slot * 12 + tile, rows, :]
                if offset > 32:
                    piece = jnp.concatenate([piece, total[slot * 12 + tile + 1, rows, :]], 1)
                pieces.append(piece[:, offset : offset + 96])
            value = jnp.concatenate(pieces, 1)
            for k in range(3):
                block[c % 2 * 3 + k, pl.ds(slot, 96, stride=2), :] = value[:, k * 128 : (k + 1) * 128]
        for r in range(8):
            for k in range(3):
                out[r * 16 + c, :, k * 128 : (k + 1) * 128] = block[
                    c % 2 * 3 + k, r * 24 : (r + 1) * 24
                ].astype(out.dtype)


def pack(own_a, own_b, up_a, down_a, up_b, down_b):
    vmem = pl.BlockSpec(memory_space=pltpu.VMEM)
    return pl.pallas_call(
        pack_body,
        out_shape=jax.ShapeDtypeStruct((128, 24, 384), jnp.bfloat16),
        in_specs=[vmem] * 6,
        out_specs=vmem,
        scratch_shapes=[
            pltpu.VMEM((24, 384, 128), jnp.float32),
            pltpu.VMEM((6, 192, 128), jnp.float32),
        ],
        compiler_params=pltpu.CompilerParams(vmem_limit_bytes=32 << 20),
        name="pack",
    )(own_a, own_b, up_a, down_a, up_b, down_b)


def finish_body(blocks, coeff, out, wide):
    step = pl.program_id(0)

    @pl.when(step == 0)
    def _():
        for k in range(3):
            wide[k] = blocks[:, k * 128 : (k + 1) * 128].astype(jnp.float32)

    per_step = out.shape[0] // 4
    for k in range(per_step):
        t = step * per_step + k
        rows = jnp.concatenate(
            [
                jnp.concatenate([wide[k, pl.ds(2 * t + s, 128, stride=24), :] for k in range(3)], 1)
                for s in range(2)
            ],
            0,
        ).astype(jnp.bfloat16)
        result = lax.dot_general(
            rows, coeff[...], (((0,), (1,)), ((), ())),
            preferred_element_type=jnp.float32,
        )
        out[4 * k : 4 * k + 4] = result.reshape(4, 96, 768).astype(out.dtype)


def finish(blocks, coeff):
    rows = 12
    return pl.pallas_call(
        finish_body,
        grid=(48 // rows,),
        out_shape=jax.ShapeDtypeStruct((48, 96, 768), jnp.bfloat16),
        in_specs=[
            pl.BlockSpec((128 * 24, 384), lambda s: (0, 0)),
            pl.BlockSpec((768, 256), lambda s: (0, 0)),
        ],
        out_specs=pl.BlockSpec((rows, 96, 768), lambda s: (s, 0, 0)),
        scratch_shapes=[pltpu.VMEM((3, 128 * 24, 128), jnp.float32)],
        compiler_params=pltpu.CompilerParams(vmem_limit_bytes=32 << 20),
        name="finish",
    )(blocks, coeff)


def add(first, *others):
    total = first.astype(jnp.float32)
    for other in others:
        total = total + other.astype(jnp.float32)
    return total.astype(jnp.bfloat16)


def local(b_three, e_occ, e_vir, c_occ, pair_list, pair_live):
    device = lax.axis_index("row") * 16 + lax.axis_index("col")
    own_a, own_b = b_three[0], b_three[1]

    right_low_a = send(own_a, "right", 1)
    right_high_b = send(own_b, "right", -1)
    right_low_b = send(own_b, "right", 1)
    right_high_a = send(own_a, "right", -1)
    info = jnp.concatenate([pair_list.reshape(1, 32), pair_live.reshape(1, 16)], 1)
    tables = [info] + [send(info, "left", step) for step in (1, -1, 2)]
    near_low_a = send(own_a, "left", 1)
    near_high_b = send(own_b, "left", -1)
    right_far_a = send(right_low_a, "right", 1)
    right_far_b = send(right_high_b, "right", -1)
    far_a = send(near_low_a, "left", 1)
    far_b = send(near_high_b, "left", -1)
    late_low_b = send(own_b, "left", 1)
    late_high_a = send(own_a, "left", -1)
    rights = (right_low_a, right_low_b, right_high_a, right_high_b, right_far_a, right_far_b)

    def partial(lefts, which, slots, dtype=jnp.bfloat16):
        chosen = [tables[k] for k in which]
        return partial_gamma(
            device.reshape(1), chosen, e_occ, b_three, lefts, slots, rights, e_vir, dtype
        )

    low_a, high_b = partial((near_low_a, near_high_b), (1, 2), (0, 1))
    up_b = send(high_b, "left", 1)
    down_a = send(low_a, "left", -1)
    sum_a, sum_b = partial((b_three, b_three), (0, 0), (0, 1), jnp.float32)
    far_a, far_b = partial((far_a, far_b), (3, 3), (0, 1))
    relay_a = send(far_a, "left", 1)
    relay_b = send(far_b, "left", -1)
    low_b, high_a = partial((late_low_b, late_high_a), (1, 2), (1, 0))
    up_a = send(add(high_a, relay_a), "left", 1)
    down_b = send(add(low_b, relay_b), "left", -1)

    blocks = pack(sum_a, sum_b, up_a, down_a, up_b, down_b)
    moved = lax.all_to_all(blocks, AXES, split_axis=0, concat_axis=0, tiled=True)
    coeff = c_occ.reshape(-1, 128, 2).transpose(0, 2, 1).reshape(-1, 256)
    return finish(moved.reshape(128 * 24, 384), coeff)


def solution(mesh):
    return jax.shard_map(
        local,
        mesh=mesh,
        in_specs=(
            P(AXES, None, None),
            P(),
            P(),
            P(),
            P(AXES, None, None),
            P(AXES, None),
        ),
        out_specs=P("row", "col", None),
        check_vma=False,
    )
```

```python
import functools

import jax
import jax.numpy as jnp
from jax import lax
from jax.experimental import pallas as pl
from jax.experimental.pallas import tpu as pltpu
from jax.sharding import PartitionSpec as P


AXES = ("row", "col")
SIDE = 4


def shifted(kind, step):
    pairs = []
    for row in range(8):
        for z in range(SIDE):
            for x in range(SIDE):
                along_x = (row % 2 == 0) == (kind == "left")
                to_z, to_x = (z, (x + step) % SIDE) if along_x else ((z + step) % SIDE, x)
                pairs.append((row * 16 + z * SIDE + x, row * 16 + to_z * SIDE + to_x))
    return pairs


def send(value, kind, step):
    return lax.ppermute(value, AXES, shifted(kind, step))


def pair_body(device, table_a, table_b, energies, levels, own, *refs, slots, picks, started):
    count = len(picks)
    lefts, refs = refs[:2], refs[2:]
    if lefts[0].shape == own.shape:
        lefts = (own.at[0], own.at[1])
    rights = []
    for n in picks:
        if n == 0:
            rights += [own.at[0], own.at[1]]
        else:
            rights += refs[:2]
            refs = refs[2:]
    begun, refs = refs[: 2 * started], refs[2 * started :]
    out_a, out_b, left_buf, right_buf, gamma, across, left_sem, right_sem = refs
    outs = (out_a, out_b)
    col = device[0] % 16
    z, x = col // SIDE, col % SIDE
    even = device[0] // 16 % 2 == 0
    columns = [
        jnp.where(even, (z + d) % SIDE * SIDE + x, z * SIDE + (x + d) % SIDE)
        for d in ((0, 3, 1, 2)[n] for n in picks)
    ]

    def entry(m):
        side, n = m // count, m % count
        right = columns[0]
        for k in range(1, count):
            right = jnp.where(n == k, columns[k], right)

        def pick(k):
            return jnp.where(side == 0, table_a[0, k], table_b[0, k])

        first, second, live = pick(right * 2), pick(right * 2 + 1), pick(32 + right)
        wanted = jnp.where(side == 0, slots[0], slots[1])
        return first, second, (live > 0) & (first % 2 == wanted)

    left_copies = [
        pltpu.make_async_copy(left, left_buf.at[s], left_sem.at[s]) for s, left in enumerate(lefts)
    ]
    for copy in left_copies:
        copy.start()
    for m in range(2 * count):
        _, second, taken = entry(m)
        for s in range(2):

            @pl.when(taken & (second % 2 == s))
            def _():
                pltpu.make_async_copy(
                    rights[2 * (m % count) + s], right_buf.at[m], right_sem.at[m]
                ).start()

    for s in range(2):
        gamma[s] = begun[s][...] if started else jnp.zeros(gamma.shape[1:], jnp.float32)
    row = levels[...].reshape(1, levels.shape[-1])
    across[...] = jnp.broadcast_to(row, across.shape).T
    for copy in left_copies:
        copy.wait()

    def step(m, carry):
        first, second, taken = entry(m)

        @pl.when(taken)
        def _():
            pltpu.make_async_copy(rights[0], right_buf.at[m], right_sem.at[m]).wait()
            right = right_buf[m]
            integrals = lax.dot_general(
                left_buf[m // count], right, (((1,), (1,)), ((), ())),
                preferred_element_type=jnp.float32,
            )
            denominator = energies[first] + energies[second] - across[...] - row
            weighted = ((2.0 * integrals - integrals.T) / denominator).astype(jnp.bfloat16)
            gamma[m // count] += jnp.dot(weighted, right, preferred_element_type=jnp.float32)

        return carry

    lax.fori_loop(0, 2 * count, step, 0)
    for s in range(2):
        outs[s][...] = gamma[s].astype(outs[s].dtype)


def partial_gamma(scalars, levels, own, lefts, slots, rights, picks, begun, out_dtype):
    virt, aux = own.shape[1:]
    slab = jax.ShapeDtypeStruct((virt, aux), out_dtype)
    hbm = pl.BlockSpec(memory_space=pltpu.HBM)
    smem = pl.BlockSpec(memory_space=pltpu.SMEM)
    vmem = pl.BlockSpec(memory_space=pltpu.VMEM)
    left_space = hbm if lefts[0] is own else vmem
    used = [slab for n in picks if n for slab in rights[n]]
    return pl.pallas_call(
        functools.partial(pair_body, slots=slots, picks=picks, started=bool(begun)),
        out_shape=(slab, slab),
        in_specs=[smem] * 4
        + [vmem, hbm]
        + [left_space] * 2
        + [hbm] * len(used)
        + [vmem] * len(begun),
        out_specs=(vmem, vmem),
        scratch_shapes=[
            pltpu.VMEM((2, virt, aux), jnp.bfloat16),
            pltpu.VMEM((2 * len(picks), virt, aux), jnp.bfloat16),
            pltpu.VMEM((2, virt, aux), jnp.float32),
            pltpu.VMEM((virt, virt), jnp.float32),
            pltpu.SemaphoreType.DMA((2,)),
            pltpu.SemaphoreType.DMA((2 * len(picks),)),
        ],
        compiler_params=pltpu.CompilerParams(vmem_limit_bytes=40 << 20),
    )(*scalars, levels, own, *lefts, *used, *begun)


def pack_body(own_a, own_b, up_a, down_a, up_b, down_b, out, total, block):
    for slot, parts in enumerate(((own_a, up_a, down_a), (own_b, up_b, down_b))):
        for k in range(12):
            lanes = slice(k * 128, (k + 1) * 128)
            own, up, down = (part[:, lanes].astype(jnp.float32) for part in parts)
            total[slot * 12 + k] = own + up + down
    for c in range(16):
        tile, offset = divmod(c * 96, 128)
        for slot in range(2):
            pieces = []
            for q in range(4):
                rows = pl.ds(q, 96, stride=4)
                piece = total[slot * 12 + tile, rows, :]
                if offset > 32:
                    piece = jnp.concatenate([piece, total[slot * 12 + tile + 1, rows, :]], 1)
                pieces.append(piece[:, offset : offset + 96])
            value = jnp.concatenate(pieces, 1)
            for k in range(3):
                block[c % 2 * 3 + k, pl.ds(slot, 96, stride=2), :] = value[:, k * 128 : (k + 1) * 128]
        for r in range(8):
            for k in range(3):
                out[r * 16 + c, :, k * 128 : (k + 1) * 128] = block[
                    c % 2 * 3 + k, r * 24 : (r + 1) * 24
                ].astype(out.dtype)


def pack(own_a, own_b, up_a, down_a, up_b, down_b):
    vmem = pl.BlockSpec(memory_space=pltpu.VMEM)
    return pl.pallas_call(
        pack_body,
        out_shape=jax.ShapeDtypeStruct((128, 24, 384), jnp.bfloat16),
        in_specs=[vmem] * 6,
        out_specs=vmem,
        scratch_shapes=[
            pltpu.VMEM((24, 384, 128), jnp.float32),
            pltpu.VMEM((6, 192, 128), jnp.float32),
        ],
        compiler_params=pltpu.CompilerParams(vmem_limit_bytes=32 << 20),
        name="pack",
    )(own_a, own_b, up_a, down_a, up_b, down_b)


def finish_body(blocks, coeff, out, wide):
    step = pl.program_id(0)

    @pl.when(step == 0)
    def _():
        for k in range(3):
            wide[k] = blocks[:, k * 128 : (k + 1) * 128].astype(jnp.float32)

    per_step = out.shape[0] // 4
    for k in range(per_step):
        t = step * per_step + k
        rows = jnp.concatenate(
            [
                jnp.concatenate([wide[k, pl.ds(2 * t + s, 128, stride=24), :] for k in range(3)], 1)
                for s in range(2)
            ],
            0,
        ).astype(jnp.bfloat16)
        result = lax.dot_general(
            rows, coeff[...], (((0,), (1,)), ((), ())),
            preferred_element_type=jnp.float32,
        )
        out[4 * k : 4 * k + 4] = result.reshape(4, 96, 768).astype(out.dtype)


def finish(blocks, coeff):
    rows = 12
    return pl.pallas_call(
        finish_body,
        grid=(48 // rows,),
        out_shape=jax.ShapeDtypeStruct((48, 96, 768), jnp.bfloat16),
        in_specs=[
            pl.BlockSpec((128 * 24, 384), lambda s: (0, 0)),
            pl.BlockSpec((768, 256), lambda s: (0, 0)),
        ],
        out_specs=pl.BlockSpec((rows, 96, 768), lambda s: (s, 0, 0)),
        scratch_shapes=[pltpu.VMEM((3, 128 * 24, 128), jnp.float32)],
        compiler_params=pltpu.CompilerParams(vmem_limit_bytes=32 << 20),
        name="finish",
    )(blocks, coeff)


def add(first, *others):
    total = first.astype(jnp.float32)
    for other in others:
        total = total + other.astype(jnp.float32)
    return total.astype(jnp.bfloat16)


def local(b_three, e_occ, e_vir, c_occ, pair_list, pair_live):
    device = lax.axis_index("row") * 16 + lax.axis_index("col")
    own_a, own_b = b_three[0], b_three[1]

    right_low_a = send(own_a, "right", 1)
    right_high_b = send(own_b, "right", -1)
    right_low_b = send(own_b, "right", 1)
    right_high_a = send(own_a, "right", -1)
    info = jnp.concatenate([pair_list.reshape(1, 32), pair_live.reshape(1, 16)], 1)
    tables = [info] + [send(info, "left", step) for step in (1, -1, 2)]
    near_low_a = send(own_a, "left", 1)
    near_high_b = send(own_b, "left", -1)
    right_far_a = send(right_low_a, "right", 1)
    right_far_b = send(right_high_b, "right", -1)
    far_a = send(near_low_a, "left", 1)
    far_b = send(near_high_b, "left", -1)
    own_a, own_b, right_far_a, right_far_b, far_a, far_b = lax.optimization_barrier(
        (own_a, own_b, right_far_a, right_far_b, far_a, far_b)
    )
    late_low_b = send(own_b, "left", 1)
    late_high_a = send(own_a, "left", -1)
    rights = (
        None,
        (right_low_a, right_low_b),
        (right_high_a, right_high_b),
        (right_far_a, right_far_b),
    )

    def partial(lefts, which, slots, dtype=jnp.bfloat16, picks=(0, 1, 2, 3), begun=()):
        scalars = [device.reshape(1)] + [tables[k] for k in which] + [e_occ]
        return partial_gamma(scalars, e_vir, b_three, lefts, slots, rights, picks, begun, dtype)

    near = (near_low_a, near_high_b)
    begun = partial(near, (1, 2), (0, 1), jnp.float32, (0, 1, 2))
    far_a, far_b = partial((far_a, far_b), (3, 3), (0, 1))
    relay_a = send(far_a, "left", 1)
    relay_b = send(far_b, "left", -1)
    low_a, high_b = partial(near, (1, 2), (0, 1), picks=(3,), begun=begun)
    low_b, high_a = partial((late_low_b, late_high_a), (1, 2), (1, 0))
    up_b = send(high_b, "left", 1)
    down_a = send(low_a, "left", -1)
    joint_a, joint_b = add(high_a, relay_a), add(low_b, relay_b)
    up_a = send(joint_a, "left", 1)
    down_b = send(joint_b, "left", -1)
    sum_a, sum_b = partial((b_three, b_three), (0, 0), (0, 1), jnp.float32)

    blocks = pack(sum_a, sum_b, up_a, down_a, up_b, down_b)
    moved = lax.all_to_all(blocks, AXES, split_axis=0, concat_axis=0, tiled=True)
    coeff = c_occ.reshape(-1, 128, 2).transpose(0, 2, 1).reshape(-1, 256)
    return finish(moved.reshape(128 * 24, 384), coeff)


def solution(mesh):
    return jax.shard_map(
        local,
        mesh=mesh,
        in_specs=(
            P(AXES, None, None),
            P(),
            P(),
            P(),
            P(AXES, None, None),
            P(AXES, None),
        ),
        out_specs=P("row", "col", None),
        check_vma=False,
    )
```

```python
import functools

import jax
import jax.numpy as jnp
from jax import lax
from jax.experimental import pallas as pl
from jax.experimental.pallas import tpu as pltpu
from jax.sharding import PartitionSpec as P


AXES = ("row", "col")
PARTS = ((0, 16), (16, 48))
SIDE = 4


def shifted(kind, step):
    pairs = []
    for row in range(8):
        for z in range(SIDE):
            for x in range(SIDE):
                along_x = (row % 2 == 0) == (kind == "left")
                to_z, to_x = (z, (x + step) % SIDE) if along_x else ((z + step) % SIDE, x)
                pairs.append((row * 16 + z * SIDE + x, row * 16 + to_z * SIDE + to_x))
    return pairs


def send(value, kind, step):
    return lax.ppermute(value, AXES, shifted(kind, step))


def pair_body(device, table_a, table_b, energies, levels, own, *refs, slots, picks, started):
    count = len(picks)
    lefts, refs = refs[:2], refs[2:]
    if lefts[0].shape == own.shape:
        lefts = (own.at[0], own.at[1])
    rights = []
    for n in picks:
        if n == 3:
            rights += refs[:2]
            refs = refs[2:]
        elif n:
            rights += [refs[0].at[0], refs[0].at[1]]
            refs = refs[1:]
        else:
            rights += [own.at[0], own.at[1]]
    begun, refs = refs[: 2 * started], refs[2 * started :]
    *outs, left_buf, right_buf, gamma, across, left_sem, right_sem = refs
    col = device[0] % 16
    z, x = col // SIDE, col % SIDE
    even = device[0] // 16 % 2 == 0
    columns = [
        jnp.where(even, (z + d) % SIDE * SIDE + x, z * SIDE + (x + d) % SIDE)
        for d in ((0, 3, 1, 2)[n] for n in picks)
    ]

    def entry(m):
        side, n = m // count, m % count
        right = columns[0]
        for k in range(1, count):
            right = jnp.where(n == k, columns[k], right)

        def pick(k):
            return jnp.where(side == 0, table_a[0, k], table_b[0, k])

        first, second, live = pick(right * 2), pick(right * 2 + 1), pick(32 + right)
        wanted = jnp.where(side == 0, slots[0], slots[1])
        return first, second, (live > 0) & (first % 2 == wanted)

    left_copies = [
        pltpu.make_async_copy(left, left_buf.at[s], left_sem.at[s]) for s, left in enumerate(lefts)
    ]
    for copy in left_copies:
        copy.start()
    for m in range(2 * count):
        _, second, taken = entry(m)
        for s in range(2):

            @pl.when(taken & (second % 2 == s))
            def _():
                pltpu.make_async_copy(
                    rights[2 * (m % count) + s], right_buf.at[m], right_sem.at[m]
                ).start()

    for s in range(2):
        gamma[s] = begun[s][...] if started else jnp.zeros(gamma.shape[1:], jnp.float32)
    row = levels[...].reshape(1, levels.shape[-1])
    across[...] = jnp.broadcast_to(row, across.shape).T
    for copy in left_copies:
        copy.wait()

    def step(m, carry):
        first, second, taken = entry(m)

        @pl.when(taken)
        def _():
            pltpu.make_async_copy(rights[0], right_buf.at[m], right_sem.at[m]).wait()
            right = right_buf[m]
            integrals = lax.dot_general(
                left_buf[m // count], right, (((1,), (1,)), ((), ())),
                preferred_element_type=jnp.float32,
            )
            denominator = energies[first] + energies[second] - across[...] - row
            weighted = ((2.0 * integrals - integrals.T) / denominator).astype(jnp.bfloat16)
            gamma[m // count] += jnp.dot(weighted, right, preferred_element_type=jnp.float32)

        return carry

    lax.fori_loop(0, 2 * count, step, 0)
    for s in range(2):
        if len(outs) == 2:
            outs[s][...] = gamma[s]
            continue
        for part, (low, high) in enumerate(PARTS):
            out = outs[2 * s + part]
            rows = high - low
            for block in range(8):
                out[block * rows : (block + 1) * rows] = gamma[
                    s, block * 48 + low : block * 48 + high
                ].astype(out.dtype)


def partial_gamma(scalars, levels, own, lefts, slots, rights, picks, begun, out_dtype, split):
    virt, aux = own.shape[1:]
    heights = [(high - low) * 8 for low, high in PARTS] if split else [virt]
    out_shape = [jax.ShapeDtypeStruct((height, aux), out_dtype) for height in heights] * 2
    hbm = pl.BlockSpec(memory_space=pltpu.HBM)
    smem = pl.BlockSpec(memory_space=pltpu.SMEM)
    vmem = pl.BlockSpec(memory_space=pltpu.VMEM)
    left_space = hbm if lefts[0] is own else vmem
    used = [slab for n in picks if n for slab in rights[n]]
    return pl.pallas_call(
        functools.partial(pair_body, slots=slots, picks=picks, started=bool(begun)),
        out_shape=out_shape,
        in_specs=[smem] * 4
        + [vmem, hbm]
        + [left_space] * 2
        + [hbm] * len(used)
        + [vmem] * len(begun),
        out_specs=[vmem] * len(out_shape),
        scratch_shapes=[
            pltpu.VMEM((2, virt, aux), jnp.bfloat16),
            pltpu.VMEM((2 * len(picks), virt, aux), jnp.bfloat16),
            pltpu.VMEM((2, virt, aux), jnp.float32),
            pltpu.VMEM((virt, virt), jnp.float32),
            pltpu.SemaphoreType.DMA((2,)),
            pltpu.SemaphoreType.DMA((2 * len(picks),)),
        ],
        compiler_params=pltpu.CompilerParams(vmem_limit_bytes=40 << 20),
    )(*scalars, levels, own, *lefts, *used, *begun)


def pack_body(own_a, own_b, up_a, down_a, up_b, down_b, out, total, block):
    height, rows = own_a.shape[0], out.shape[1]
    for slot, parts in enumerate(((own_a, up_a, down_a), (own_b, up_b, down_b))):
        for k in range(12):
            lanes = slice(k * 128, (k + 1) * 128)
            own, up, down = (part[:, lanes].astype(jnp.float32) for part in parts)
            total[slot * 12 + k] = own + up + down
    for c in range(16):
        tile, offset = divmod(c * 96, 128)
        for slot in range(2):
            pieces = []
            for q in range(4):
                picked = pl.ds(q, height // 4, stride=4)
                piece = total[slot * 12 + tile, picked, :]
                if offset > 32:
                    piece = jnp.concatenate([piece, total[slot * 12 + tile + 1, picked, :]], 1)
                pieces.append(piece[:, offset : offset + 96])
            value = jnp.concatenate(pieces, 1)
            for k in range(3):
                block[c % 2 * 3 + k, pl.ds(slot, height // 4, stride=2), :] = value[
                    :, k * 128 : (k + 1) * 128
                ]
        for r in range(8):
            for k in range(3):
                out[r * 16 + c, :, k * 128 : (k + 1) * 128] = block[
                    c % 2 * 3 + k, r * rows : (r + 1) * rows
                ].astype(out.dtype)


def pack(own_a, own_b, up_a, down_a, up_b, down_b):
    height = own_a.shape[0]
    vmem = pl.BlockSpec(memory_space=pltpu.VMEM)
    return pl.pallas_call(
        pack_body,
        out_shape=jax.ShapeDtypeStruct((128, height // 16, 384), jnp.bfloat16),
        in_specs=[vmem] * 6,
        out_specs=vmem,
        scratch_shapes=[
            pltpu.VMEM((24, height, 128), jnp.float32),
            pltpu.VMEM((6, height // 2, 128), jnp.float32),
        ],
        compiler_params=pltpu.CompilerParams(vmem_limit_bytes=32 << 20),
    )(own_a, own_b, up_a, down_a, up_b, down_b)


def finish_body(tail, head, coeff, out, wide_tail, wide_head):
    step = pl.program_id(0)

    def run(wide, stride, first):
        for k in range(4):
            picked = [pl.ds(first + 2 * k + s, 128, stride=stride) for s in range(2)]
            rows = jnp.concatenate(
                [jnp.concatenate([wide[lane, rows, :] for lane in range(3)], 1) for rows in picked], 0
            ).astype(jnp.bfloat16)
            result = lax.dot_general(
                rows, coeff[...], (((0,), (1,)), ((), ())), preferred_element_type=jnp.float32
            )
            out[4 * k : 4 * k + 4] = result.reshape(4, 96, 768).astype(out.dtype)

    @pl.when(step == 0)
    def _():
        for k in range(3):
            wide_head[k] = head[:, k * 128 : (k + 1) * 128].astype(jnp.float32)
            wide_tail[k] = tail[:, k * 128 : (k + 1) * 128].astype(jnp.float32)
        run(wide_head, 8, 0)

    @pl.when(step > 0)
    def _():
        run(wide_tail, 16, 8 * step - 8)


def finish(tail, head, coeff):
    whole = lambda s: (0, 0)
    return pl.pallas_call(
        finish_body,
        grid=(3,),
        out_shape=jax.ShapeDtypeStruct((48, 96, 768), jnp.bfloat16),
        in_specs=[
            pl.BlockSpec((128 * 16, 384), whole),
            pl.BlockSpec((128 * 8, 384), whole),
            pl.BlockSpec((768, 256), whole),
        ],
        out_specs=pl.BlockSpec((16, 96, 768), lambda s: (s, 0, 0)),
        scratch_shapes=[
            pltpu.VMEM((3, 128 * 16, 128), jnp.float32),
            pltpu.VMEM((3, 128 * 8, 128), jnp.float32),
        ],
        compiler_params=pltpu.CompilerParams(vmem_limit_bytes=32 << 20),
        name="finish",
    )(tail, head, coeff)


def add(first, *others):
    total = first.astype(jnp.float32)
    for other in others:
        total = total + other.astype(jnp.float32)
    return total.astype(jnp.bfloat16)


def local(b_three, e_occ, e_vir, c_occ, pair_list, pair_live):
    device = lax.axis_index("row") * 16 + lax.axis_index("col")

    right_low = send(b_three, "right", 1)
    right_high = send(b_three, "right", -1)
    own_a, own_b = b_three[0], b_three[1]
    info = jnp.concatenate([pair_list.reshape(1, 32), pair_live.reshape(1, 16)], 1)
    tables = [info] + [send(info, "left", step) for step in (1, -1, 2)]
    near_low_a = send(own_a, "left", 1)
    near_high_b = send(own_b, "left", -1)
    right_far_a = send(right_low[0], "right", 1)
    right_far_b = send(right_high[1], "right", -1)
    far_a = send(near_low_a, "left", 1)
    far_b = send(near_high_b, "left", -1)
    own_a, own_b, right_far_a, right_far_b, far_a, far_b = lax.optimization_barrier(
        (own_a, own_b, right_far_a, right_far_b, far_a, far_b)
    )
    late_low_b = send(own_b, "left", 1)
    late_high_a = send(own_a, "left", -1)
    rights = ((), (right_low,), (right_high,), (right_far_a, right_far_b))

    def partial(lefts, which, slots, dtype=jnp.bfloat16, picks=(0, 1, 2, 3), begun=(), split=True):
        scalars = [device.reshape(1)] + [tables[k] for k in which] + [e_occ]
        return partial_gamma(
            scalars, e_vir, b_three, lefts, slots, rights, picks, begun, dtype, split
        )

    near = (near_low_a, near_high_b)
    begun = partial(near, (1, 2), (0, 1), jnp.float32, (0, 1, 2), split=False)
    far = partial((far_a, far_b), (3, 3), (0, 1))
    relay = [send(far[k], "left", 1 if k < 2 else -1) for k in range(4)]
    rest = partial(near, (1, 2), (0, 1), picks=(3,), begun=begun)
    late = partial((late_low_b, late_high_a), (1, 2), (1, 0))
    sums = partial((b_three, b_three), (0, 0), (0, 1), jnp.float32)
    moved = []
    for k in range(2):
        up_b = send(rest[2 + k], "left", 1)
        down_a = send(rest[k], "left", -1)
        joint_a, joint_b = add(late[2 + k], relay[k]), add(late[k], relay[2 + k])
        up_a = send(joint_a, "left", 1)
        down_b = send(joint_b, "left", -1)
        blocks = pack(sums[k], sums[2 + k], up_a, down_a, up_b, down_b)
        blocks = lax.all_to_all(blocks, AXES, split_axis=0, concat_axis=0, tiled=True)
        moved.append(blocks.reshape(-1, 384))
    coeff = c_occ.reshape(-1, 128, 2).transpose(0, 2, 1).reshape(-1, 256)
    return finish(moved[1], moved[0], coeff)


def solution(mesh):
    return jax.shard_map(
        local,
        mesh=mesh,
        in_specs=(
            P(AXES, None, None),
            P(),
            P(),
            P(),
            P(AXES, None, None),
            P(AXES, None),
        ),
        out_specs=P("row", "col", None),
        check_vma=False,
    )
```

```python
import functools

import jax
import jax.numpy as jnp
from jax import lax
from jax.experimental import pallas as pl
from jax.experimental.pallas import tpu as pltpu
from jax.sharding import PartitionSpec as P


AXES = ("row", "col")
SIDE = 4


def shifted(kind, step):
    pairs = []
    for row in range(8):
        for z in range(SIDE):
            for x in range(SIDE):
                along_x = (row % 2 == 0) == (kind == "left")
                to_z, to_x = (z, (x + step) % SIDE) if along_x else ((z + step) % SIDE, x)
                pairs.append((row * 16 + z * SIDE + x, row * 16 + to_z * SIDE + to_x))
    return pairs


def send(value, kind, step):
    return lax.ppermute(value, AXES, shifted(kind, step))


def pair_body(device, table_a, table_b, energies, levels, own, *refs, slots, picks, started):
    count = len(picks)
    lefts, refs = refs[:2], refs[2:]
    if lefts[0].shape == own.shape:
        lefts = (own.at[0], own.at[1])
    rights = []
    for n in picks:
        if n == 3:
            rights += refs[:2]
            refs = refs[2:]
        elif n:
            rights += [refs[0].at[0], refs[0].at[1]]
            refs = refs[1:]
        else:
            rights += [own.at[0], own.at[1]]
    begun, refs = refs[: 2 * started], refs[2 * started :]
    out_a, out_b, left_buf, right_buf, gamma, across, left_sem, right_sem = refs
    outs = (out_a, out_b)
    col = device[0] % 16
    z, x = col // SIDE, col % SIDE
    even = device[0] // 16 % 2 == 0
    columns = [
        jnp.where(even, (z + d) % SIDE * SIDE + x, z * SIDE + (x + d) % SIDE)
        for d in ((0, 3, 1, 2)[n] for n in picks)
    ]

    def entry(m):
        side, n = m // count, m % count
        right = columns[0]
        for k in range(1, count):
            right = jnp.where(n == k, columns[k], right)

        def pick(k):
            return jnp.where(side == 0, table_a[0, k], table_b[0, k])

        first, second, live = pick(right * 2), pick(right * 2 + 1), pick(32 + right)
        wanted = jnp.where(side == 0, slots[0], slots[1])
        return first, second, (live > 0) & (first % 2 == wanted)

    left_copies = [
        pltpu.make_async_copy(left, left_buf.at[s], left_sem.at[s]) for s, left in enumerate(lefts)
    ]
    for copy in left_copies:
        copy.start()
    for m in range(2 * count):
        _, second, taken = entry(m)
        for s in range(2):

            @pl.when(taken & (second % 2 == s))
            def _():
                pltpu.make_async_copy(
                    rights[2 * (m % count) + s], right_buf.at[m], right_sem.at[m]
                ).start()

    for s in range(2):
        gamma[s] = begun[s][...] if started else jnp.zeros(gamma.shape[1:], jnp.float32)
    row = levels[...].reshape(1, levels.shape[-1])
    across[...] = jnp.broadcast_to(row, across.shape).T
    for copy in left_copies:
        copy.wait()

    def step(m, carry):
        first, second, taken = entry(m)

        @pl.when(taken)
        def _():
            pltpu.make_async_copy(rights[0], right_buf.at[m], right_sem.at[m]).wait()
            right = right_buf[m]
            integrals = lax.dot_general(
                left_buf[m // count], right, (((1,), (1,)), ((), ())),
                preferred_element_type=jnp.float32,
            )
            denominator = energies[first] + energies[second] - across[...] - row
            weighted = ((2.0 * integrals - integrals.T) / denominator).astype(jnp.bfloat16)
            gamma[m // count] += jnp.dot(weighted, right, preferred_element_type=jnp.float32)

        return carry

    lax.fori_loop(0, 2 * count, step, 0)
    for s in range(2):
        outs[s][...] = gamma[s].astype(outs[s].dtype)


def partial_gamma(scalars, levels, own, lefts, slots, rights, picks, begun, out_dtype):
    virt, aux = own.shape[1:]
    slab = jax.ShapeDtypeStruct((virt, aux), out_dtype)
    hbm = pl.BlockSpec(memory_space=pltpu.HBM)
    smem = pl.BlockSpec(memory_space=pltpu.SMEM)
    vmem = pl.BlockSpec(memory_space=pltpu.VMEM)
    left_space = hbm if lefts[0] is own else vmem
    used = [slab for n in picks if n for slab in rights[n]]
    return pl.pallas_call(
        functools.partial(pair_body, slots=slots, picks=picks, started=bool(begun)),
        out_shape=(slab, slab),
        in_specs=[smem] * 4
        + [vmem, hbm]
        + [left_space] * 2
        + [hbm] * len(used)
        + [vmem] * len(begun),
        out_specs=(vmem, vmem),
        scratch_shapes=[
            pltpu.VMEM((2, virt, aux), jnp.bfloat16),
            pltpu.VMEM((2 * len(picks), virt, aux), jnp.bfloat16),
            pltpu.VMEM((2, virt, aux), jnp.float32),
            pltpu.VMEM((virt, virt), jnp.float32),
            pltpu.SemaphoreType.DMA((2,)),
            pltpu.SemaphoreType.DMA((2 * len(picks),)),
        ],
        compiler_params=pltpu.CompilerParams(vmem_limit_bytes=40 << 20),
    )(*scalars, levels, own, *lefts, *used, *begun)


def pack_body(own_a, own_b, up_a, down_a, up_b, down_b, out, total, block):
    for slot, parts in enumerate(((own_a, up_a, down_a), (own_b, up_b, down_b))):
        for k in range(12):
            lanes = slice(k * 128, (k + 1) * 128)
            own, up, down = (part[:, lanes].astype(jnp.float32) for part in parts)
            total[slot * 12 + k] = own + up + down
    for c in range(16):
        tile, offset = divmod(c * 96, 128)
        for slot in range(2):
            pieces = []
            for q in range(4):
                rows = pl.ds(q, 96, stride=4)
                piece = total[slot * 12 + tile, rows, :]
                if offset > 32:
                    piece = jnp.concatenate([piece, total[slot * 12 + tile + 1, rows, :]], 1)
                pieces.append(piece[:, offset : offset + 96])
            value = jnp.concatenate(pieces, 1)
            for k in range(3):
                block[c % 2 * 3 + k, pl.ds(slot, 96, stride=2), :] = value[:, k * 128 : (k + 1) * 128]
        for r in range(8):
            for k in range(3):
                out[r * 16 + c, :, k * 128 : (k + 1) * 128] = block[
                    c % 2 * 3 + k, r * 24 : (r + 1) * 24
                ].astype(out.dtype)


def pack(own_a, own_b, up_a, down_a, up_b, down_b):
    vmem = pl.BlockSpec(memory_space=pltpu.VMEM)
    return pl.pallas_call(
        pack_body,
        out_shape=jax.ShapeDtypeStruct((128, 24, 384), jnp.bfloat16),
        in_specs=[vmem] * 6,
        out_specs=vmem,
        scratch_shapes=[
            pltpu.VMEM((24, 384, 128), jnp.float32),
            pltpu.VMEM((6, 192, 128), jnp.float32),
        ],
        compiler_params=pltpu.CompilerParams(vmem_limit_bytes=20 << 20),
        name="pack",
    )(own_a, own_b, up_a, down_a, up_b, down_b)


def finish_body(blocks, coeff, out, wide):
    step = pl.program_id(0)

    @pl.when(step == 0)
    def _():
        for k in range(3):
            wide[k] = blocks[:, k * 128 : (k + 1) * 128].astype(jnp.float32)

    per_step = out.shape[0] // 4
    for k in range(per_step):
        t = step * per_step + k
        rows = jnp.concatenate(
            [
                jnp.concatenate([wide[k, pl.ds(2 * t + s, 128, stride=24), :] for k in range(3)], 1)
                for s in range(2)
            ],
            0,
        ).astype(jnp.bfloat16)
        result = lax.dot_general(
            rows, coeff[...], (((0,), (1,)), ((), ())),
            preferred_element_type=jnp.float32,
        )
        out[4 * k : 4 * k + 4] = result.reshape(4, 96, 768).astype(out.dtype)


def finish(blocks, coeff):
    rows = 12
    return pl.pallas_call(
        finish_body,
        grid=(48 // rows,),
        out_shape=jax.ShapeDtypeStruct((48, 96, 768), jnp.bfloat16),
        in_specs=[
            pl.BlockSpec((128 * 24, 384), lambda s: (0, 0)),
            pl.BlockSpec((768, 256), lambda s: (0, 0)),
        ],
        out_specs=pl.BlockSpec((rows, 96, 768), lambda s: (s, 0, 0)),
        scratch_shapes=[pltpu.VMEM((3, 128 * 24, 128), jnp.float32)],
        compiler_params=pltpu.CompilerParams(vmem_limit_bytes=20 << 20),
        name="finish",
    )(blocks, coeff)


def add(first, *others):
    total = first.astype(jnp.float32)
    for other in others:
        total = total + other.astype(jnp.float32)
    return total.astype(jnp.bfloat16)


def local(b_three, e_occ, e_vir, c_occ, pair_list, pair_live):
    device = lax.axis_index("row") * 16 + lax.axis_index("col")

    right_low = send(b_three, "right", 1)
    right_high = send(b_three, "right", -1)
    own_a, own_b = b_three[0], b_three[1]
    info = jnp.concatenate([pair_list.reshape(1, 32), pair_live.reshape(1, 16)], 1)
    tables = [info] + [send(info, "left", step) for step in (1, -1, 2)]
    near_low_a = send(own_a, "left", 1)
    near_high_b = send(own_b, "left", -1)
    right_far_a = send(right_low[0], "right", 1)
    right_far_b = send(right_high[1], "right", -1)
    far_a = send(near_low_a, "left", 1)
    far_b = send(near_high_b, "left", -1)
    own_a, own_b, right_far_a, right_far_b, far_a, far_b = lax.optimization_barrier(
        (own_a, own_b, right_far_a, right_far_b, far_a, far_b)
    )
    late_low_b = send(own_b, "left", 1)
    late_high_a = send(own_a, "left", -1)
    rights = ((), (right_low,), (right_high,), (right_far_a, right_far_b))

    def partial(lefts, which, slots, dtype=jnp.bfloat16, picks=(0, 1, 2, 3), begun=()):
        scalars = [device.reshape(1)] + [tables[k] for k in which] + [e_occ]
        return partial_gamma(scalars, e_vir, b_three, lefts, slots, rights, picks, begun, dtype)

    near = (near_low_a, near_high_b)
    begun = partial(near, (1, 2), (0, 1), jnp.float32, (0, 1, 2))
    far_a, far_b = partial((far_a, far_b), (3, 3), (0, 1))
    relay_a = send(far_a, "left", 1)
    relay_b = send(far_b, "left", -1)
    low_b, high_a = partial((late_low_b, late_high_a), (1, 2), (1, 0))
    up_a = send(add(high_a, relay_a), "left", 1)
    down_b = send(add(low_b, relay_b), "left", -1)
    low_a, high_b = partial(near, (1, 2), (0, 1), picks=(3,), begun=begun)
    up_b = send(high_b, "left", 1)
    down_a = send(low_a, "left", -1)
    sum_a, sum_b = partial((b_three, b_three), (0, 0), (0, 1), jnp.float32)

    blocks = pack(sum_a, sum_b, up_a, down_a, up_b, down_b)
    moved = lax.all_to_all(blocks, AXES, split_axis=0, concat_axis=0, tiled=True)
    coeff = c_occ.reshape(-1, 128, 2).transpose(0, 2, 1).reshape(-1, 256)
    return finish(moved.reshape(128 * 24, 384), coeff)


def solution(mesh):
    return jax.shard_map(
        local,
        mesh=mesh,
        in_specs=(
            P(AXES, None, None),
            P(),
            P(),
            P(),
            P(AXES, None, None),
            P(AXES, None),
        ),
        out_specs=P("row", "col", None),
        check_vma=False,
    )
```

```python
import functools

import jax
import jax.numpy as jnp
from jax import lax
from jax.experimental import pallas as pl
from jax.experimental.pallas import tpu as pltpu
from jax.sharding import PartitionSpec as P


AXES = ("row", "col")
SIDE = 4


def shifted(kind, step):
    pairs = []
    for row in range(8):
        for z in range(SIDE):
            for x in range(SIDE):
                along_x = (row % 2 == 0) == (kind == "left")
                to_z, to_x = (z, (x + step) % SIDE) if along_x else ((z + step) % SIDE, x)
                pairs.append((row * 16 + z * SIDE + x, row * 16 + to_z * SIDE + to_x))
    return pairs


def send(value, kind, step):
    return lax.ppermute(value, AXES, shifted(kind, step))


def pair_body(device, table_a, table_b, energies, levels, own, *refs, slots, picks, started):
    count = len(picks)
    lefts, refs = refs[:2], refs[2:]
    if lefts[0].shape == own.shape:
        lefts = (own.at[0], own.at[1])
    rights = []
    for n in picks:
        if n == 3:
            rights += refs[:2]
            refs = refs[2:]
        elif n:
            rights += [refs[0].at[0], refs[0].at[1]]
            refs = refs[1:]
        else:
            rights += [own.at[0], own.at[1]]
    begun, refs = refs[: 2 * started], refs[2 * started :]
    out_a, out_b, left_buf, right_buf, gamma, across, left_sem, right_sem = refs
    outs = (out_a, out_b)
    col = device[0] % 16
    z, x = col // SIDE, col % SIDE
    even = device[0] // 16 % 2 == 0
    columns = [
        jnp.where(even, (z + d) % SIDE * SIDE + x, z * SIDE + (x + d) % SIDE)
        for d in ((0, 3, 1, 2)[n] for n in picks)
    ]

    def entry(m):
        side, n = m // count, m % count
        right = columns[0]
        for k in range(1, count):
            right = jnp.where(n == k, columns[k], right)

        def pick(k):
            return jnp.where(side == 0, table_a[0, k], table_b[0, k])

        first, second, live = pick(right * 2), pick(right * 2 + 1), pick(32 + right)
        wanted = jnp.where(side == 0, slots[0], slots[1])
        return first, second, (live > 0) & (first % 2 == wanted)

    left_copies = [
        pltpu.make_async_copy(left, left_buf.at[s], left_sem.at[s]) for s, left in enumerate(lefts)
    ]
    for copy in left_copies:
        copy.start()
    for m in range(2 * count):
        _, second, taken = entry(m)
        for s in range(2):

            @pl.when(taken & (second % 2 == s))
            def _():
                pltpu.make_async_copy(
                    rights[2 * (m % count) + s], right_buf.at[m], right_sem.at[m]
                ).start()

    for s in range(2):
        gamma[s] = begun[s][...] if started else jnp.zeros(gamma.shape[1:], jnp.float32)
    row = levels[...].reshape(1, levels.shape[-1])
    across[...] = jnp.broadcast_to(row, across.shape).T
    for copy in left_copies:
        copy.wait()

    def step(m, carry):
        first, second, taken = entry(m)

        @pl.when(taken)
        def _():
            pltpu.make_async_copy(rights[0], right_buf.at[m], right_sem.at[m]).wait()
            right = right_buf[m]
            integrals = lax.dot_general(
                left_buf[m // count], right, (((1,), (1,)), ((), ())),
                preferred_element_type=jnp.float32,
            )
            denominator = energies[first] + energies[second] - across[...] - row
            weighted = ((2.0 * integrals - integrals.T) / denominator).astype(jnp.bfloat16)
            gamma[m // count] += jnp.dot(weighted, right, preferred_element_type=jnp.float32)

        return carry

    lax.fori_loop(0, 2 * count, step, 0)
    for s in range(2):
        outs[s][...] = gamma[s].astype(outs[s].dtype)


def partial_gamma(scalars, levels, own, lefts, slots, rights, picks, begun, out_dtype):
    virt, aux = own.shape[1:]
    slab = jax.ShapeDtypeStruct((virt, aux), out_dtype)
    hbm = pl.BlockSpec(memory_space=pltpu.HBM)
    smem = pl.BlockSpec(memory_space=pltpu.SMEM)
    vmem = pl.BlockSpec(memory_space=pltpu.VMEM)
    left_space = hbm if lefts[0] is own else vmem
    used = [slab for n in picks if n for slab in rights[n]]
    return pl.pallas_call(
        functools.partial(pair_body, slots=slots, picks=picks, started=bool(begun)),
        out_shape=(slab, slab),
        in_specs=[smem] * 4
        + [vmem, hbm]
        + [left_space] * 2
        + [hbm] * len(used)
        + [vmem] * len(begun),
        out_specs=(vmem, vmem),
        scratch_shapes=[
            pltpu.VMEM((2, virt, aux), jnp.bfloat16),
            pltpu.VMEM((2 * len(picks), virt, aux), jnp.bfloat16),
            pltpu.VMEM((2, virt, aux), jnp.float32),
            pltpu.VMEM((virt, virt), jnp.float32),
            pltpu.SemaphoreType.DMA((2,)),
            pltpu.SemaphoreType.DMA((2 * len(picks),)),
        ],
        compiler_params=pltpu.CompilerParams(vmem_limit_bytes=40 << 20),
    )(*scalars, levels, own, *lefts, *used, *begun)


def pack_body(own_a, own_b, up_a, down_a, up_b, down_b, out, total, block):
    for slot, parts in enumerate(((own_a, up_a, down_a), (own_b, up_b, down_b))):
        for k in range(12):
            lanes = slice(k * 128, (k + 1) * 128)
            own, up, down = (part[:, lanes].astype(jnp.float32) for part in parts)
            total[slot * 12 + k] = own + up + down
    for c in range(16):
        tile, offset = divmod(c * 96, 128)
        for slot in range(2):
            pieces = []
            for q in range(4):
                rows = pl.ds(q, 96, stride=4)
                piece = total[slot * 12 + tile, rows, :]
                if offset > 32:
                    piece = jnp.concatenate([piece, total[slot * 12 + tile + 1, rows, :]], 1)
                pieces.append(piece[:, offset : offset + 96])
            value = jnp.concatenate(pieces, 1)
            for k in range(3):
                block[c % 2 * 3 + k, pl.ds(slot, 96, stride=2), :] = value[:, k * 128 : (k + 1) * 128]
        for r in range(8):
            for k in range(3):
                out[r * 16 + c, :, k * 128 : (k + 1) * 128] = block[
                    c % 2 * 3 + k, r * 24 : (r + 1) * 24
                ].astype(out.dtype)


def pack(own_a, own_b, up_a, down_a, up_b, down_b):
    vmem = pl.BlockSpec(memory_space=pltpu.VMEM)
    return pl.pallas_call(
        pack_body,
        out_shape=jax.ShapeDtypeStruct((128, 24, 384), jnp.bfloat16),
        in_specs=[vmem] * 6,
        out_specs=vmem,
        scratch_shapes=[
            pltpu.VMEM((24, 384, 128), jnp.float32),
            pltpu.VMEM((6, 192, 128), jnp.float32),
        ],
        compiler_params=pltpu.CompilerParams(vmem_limit_bytes=20 << 20),
        name="pack",
    )(own_a, own_b, up_a, down_a, up_b, down_b)


def finish_body(blocks, coeff, out, wide):
    step = pl.program_id(0)

    @pl.when(step == 0)
    def _():
        for k in range(3):
            wide[k] = blocks[:, k * 128 : (k + 1) * 128].astype(jnp.float32)

    per_step = out.shape[0] // 4
    for k in range(per_step):
        t = step * per_step + k
        rows = jnp.concatenate(
            [
                jnp.concatenate([wide[k, pl.ds(2 * t + s, 128, stride=24), :] for k in range(3)], 1)
                for s in range(2)
            ],
            0,
        ).astype(jnp.bfloat16)
        result = lax.dot_general(
            rows, coeff[...], (((0,), (1,)), ((), ())),
            preferred_element_type=jnp.float32,
        )
        out[4 * k : 4 * k + 4] = result.reshape(4, 96, 768).astype(out.dtype)


def finish(blocks, coeff):
    rows = 12
    return pl.pallas_call(
        finish_body,
        grid=(48 // rows,),
        out_shape=jax.ShapeDtypeStruct((48, 96, 768), jnp.bfloat16),
        in_specs=[
            pl.BlockSpec((128 * 24, 384), lambda s: (0, 0)),
            pl.BlockSpec((768, 256), lambda s: (0, 0)),
        ],
        out_specs=pl.BlockSpec((rows, 96, 768), lambda s: (s, 0, 0)),
        scratch_shapes=[pltpu.VMEM((3, 128 * 24, 128), jnp.float32)],
        compiler_params=pltpu.CompilerParams(vmem_limit_bytes=20 << 20),
        name="finish",
    )(blocks, coeff)


def split_body(low, high, out_a, out_b, sems):
    copies = [
        pltpu.make_async_copy(low.at[0], out_a, sems.at[0]),
        pltpu.make_async_copy(high.at[1], out_b, sems.at[1]),
    ]
    for copy in copies:
        copy.start()
    for copy in copies:
        copy.wait()


def split(low, high):
    slab = jax.ShapeDtypeStruct(low.shape[1:], low.dtype)
    hbm = pl.BlockSpec(memory_space=pltpu.HBM)
    return pl.pallas_call(
        split_body,
        out_shape=(slab, slab),
        in_specs=[hbm, hbm],
        out_specs=(hbm, hbm),
        scratch_shapes=[pltpu.SemaphoreType.DMA((2,))],
        compiler_params=pltpu.CompilerParams(vmem_limit_bytes=60 << 20),
        name="split",
    )(low, high)


def add(first, *others):
    total = first.astype(jnp.float32)
    for other in others:
        total = total + other.astype(jnp.float32)
    return total.astype(jnp.bfloat16)


def local(b_three, e_occ, e_vir, c_occ, pair_list, pair_live):
    device = lax.axis_index("row") * 16 + lax.axis_index("col")

    right_low = send(b_three, "right", 1)
    right_high = send(b_three, "right", -1)
    own_a, own_b = b_three[0], b_three[1]
    info = jnp.concatenate([pair_list.reshape(1, 32), pair_live.reshape(1, 16)], 1)
    tables = [info] + [send(info, "left", step) for step in (1, -1, 2)]
    near_low_a = send(own_a, "left", 1)
    near_high_b = send(own_b, "left", -1)
    onward_a, onward_b = split(right_low, right_high)
    right_far_a = send(onward_a, "right", 1)
    right_far_b = send(onward_b, "right", -1)
    far_a = send(near_low_a, "left", 1)
    far_b = send(near_high_b, "left", -1)
    own_a, own_b, right_far_a, right_far_b, far_a, far_b = lax.optimization_barrier(
        (own_a, own_b, right_far_a, right_far_b, far_a, far_b)
    )
    late_low_b = send(own_b, "left", 1)
    late_high_a = send(own_a, "left", -1)
    rights = ((), (right_low,), (right_high,), (right_far_a, right_far_b))

    def partial(lefts, which, slots, dtype=jnp.bfloat16, picks=(0, 1, 2, 3), begun=()):
        scalars = [device.reshape(1)] + [tables[k] for k in which] + [e_occ]
        return partial_gamma(scalars, e_vir, b_three, lefts, slots, rights, picks, begun, dtype)

    near = (near_low_a, near_high_b)
    begun = partial(near, (1, 2), (0, 1), jnp.float32, (0, 1, 2))
    far_a, far_b = partial((far_a, far_b), (3, 3), (0, 1))
    relay_a = send(far_a, "left", 1)
    relay_b = send(far_b, "left", -1)
    low_b, high_a = partial((late_low_b, late_high_a), (1, 2), (1, 0))
    up_a = send(add(high_a, relay_a), "left", 1)
    down_b = send(add(low_b, relay_b), "left", -1)
    low_a, high_b = partial(near, (1, 2), (0, 1), picks=(3,), begun=begun)
    up_b = send(high_b, "left", 1)
    down_a = send(low_a, "left", -1)
    sum_a, sum_b = partial((b_three, b_three), (0, 0), (0, 1), jnp.float32)

    blocks = pack(sum_a, sum_b, up_a, down_a, up_b, down_b)
    moved = lax.all_to_all(blocks, AXES, split_axis=0, concat_axis=0, tiled=True)
    coeff = c_occ.reshape(-1, 128, 2).transpose(0, 2, 1).reshape(-1, 256)
    return finish(moved.reshape(128 * 24, 384), coeff)


def solution(mesh):
    return jax.shard_map(
        local,
        mesh=mesh,
        in_specs=(
            P(AXES, None, None),
            P(),
            P(),
            P(),
            P(AXES, None, None),
            P(AXES, None),
        ),
        out_specs=P("row", "col", None),
        check_vma=False,
    )
```

```python
import functools

import jax
import jax.numpy as jnp
from jax import lax
from jax.experimental import pallas as pl
from jax.experimental.pallas import tpu as pltpu
from jax.sharding import PartitionSpec as P


AXES = ("row", "col")
SIDE = 4


def shifted(kind, step):
    pairs = []
    for row in range(8):
        for z in range(SIDE):
            for x in range(SIDE):
                along_x = (row % 2 == 0) == (kind == "left")
                to_z, to_x = (z, (x + step) % SIDE) if along_x else ((z + step) % SIDE, x)
                pairs.append((row * 16 + z * SIDE + x, row * 16 + to_z * SIDE + to_x))
    return pairs


def send(value, kind, step):
    return lax.ppermute(value, AXES, shifted(kind, step))


def pair_body(device, table_a, table_b, energies, levels, own, *refs, slots, picks, started):
    count = len(picks)
    lefts, refs = refs[:2], refs[2:]
    if lefts[0].shape == own.shape:
        lefts = (own.at[0], own.at[1])
    rights = []
    for n in picks:
        if n == 3:
            rights += refs[:2]
            refs = refs[2:]
        elif n:
            rights += [refs[0].at[0], refs[0].at[1]]
            refs = refs[1:]
        else:
            rights += [own.at[0], own.at[1]]
    begun, refs = refs[: 2 * started], refs[2 * started :]
    out_a, out_b, left_buf, right_buf, gamma, across, left_sem, right_sem = refs
    outs = (out_a, out_b)
    col = device[0] % 16
    z, x = col // SIDE, col % SIDE
    even = device[0] // 16 % 2 == 0
    columns = [
        jnp.where(even, (z + d) % SIDE * SIDE + x, z * SIDE + (x + d) % SIDE)
        for d in ((0, 3, 1, 2)[n] for n in picks)
    ]

    def entry(m):
        side, n = m // count, m % count
        right = columns[0]
        for k in range(1, count):
            right = jnp.where(n == k, columns[k], right)

        def pick(k):
            return jnp.where(side == 0, table_a[0, k], table_b[0, k])

        first, second, live = pick(right * 2), pick(right * 2 + 1), pick(32 + right)
        wanted = jnp.where(side == 0, slots[0], slots[1])
        return first, second, (live > 0) & (first % 2 == wanted)

    left_copies = [
        pltpu.make_async_copy(left, left_buf.at[s], left_sem.at[s]) for s, left in enumerate(lefts)
    ]
    for copy in left_copies:
        copy.start()
    for m in range(2 * count):
        _, second, taken = entry(m)
        for s in range(2):

            @pl.when(taken & (second % 2 == s))
            def _():
                pltpu.make_async_copy(
                    rights[2 * (m % count) + s], right_buf.at[m], right_sem.at[m]
                ).start()

    for s in range(2):
        gamma[s] = begun[s][...] if started else jnp.zeros(gamma.shape[1:], jnp.float32)
    row = levels[...].reshape(1, levels.shape[-1])
    across[...] = jnp.broadcast_to(row, across.shape).T
    for copy in left_copies:
        copy.wait()

    def step(m, carry):
        first, second, taken = entry(m)

        @pl.when(taken)
        def _():
            pltpu.make_async_copy(rights[0], right_buf.at[m], right_sem.at[m]).wait()
            right = right_buf[m]
            integrals = lax.dot_general(
                left_buf[m // count], right, (((1,), (1,)), ((), ())),
                preferred_element_type=jnp.float32,
            )
            denominator = energies[first] + energies[second] - across[...] - row
            weighted = ((2.0 * integrals - integrals.T) / denominator).astype(jnp.bfloat16)
            gamma[m // count] += jnp.dot(weighted, right, preferred_element_type=jnp.float32)

        return carry

    lax.fori_loop(0, 2 * count, step, 0)
    for s in range(2):
        outs[s][...] = gamma[s].astype(outs[s].dtype)


def partial_gamma(scalars, levels, own, lefts, slots, rights, picks, begun, out_dtype):
    virt, aux = own.shape[1:]
    slab = jax.ShapeDtypeStruct((virt, aux), out_dtype)
    hbm = pl.BlockSpec(memory_space=pltpu.HBM)
    smem = pl.BlockSpec(memory_space=pltpu.SMEM)
    vmem = pl.BlockSpec(memory_space=pltpu.VMEM)
    left_space = hbm if lefts[0] is own else vmem
    used = [slab for n in picks if n for slab in rights[n]]
    return pl.pallas_call(
        functools.partial(pair_body, slots=slots, picks=picks, started=bool(begun)),
        out_shape=(slab, slab),
        in_specs=[smem] * 4
        + [vmem, hbm]
        + [left_space] * 2
        + [hbm] * len(used)
        + [vmem] * len(begun),
        out_specs=(vmem, vmem),
        scratch_shapes=[
            pltpu.VMEM((2, virt, aux), jnp.bfloat16),
            pltpu.VMEM((2 * len(picks), virt, aux), jnp.bfloat16),
            pltpu.VMEM((2, virt, aux), jnp.float32),
            pltpu.VMEM((virt, virt), jnp.float32),
            pltpu.SemaphoreType.DMA((2,)),
            pltpu.SemaphoreType.DMA((2 * len(picks),)),
        ],
        compiler_params=pltpu.CompilerParams(vmem_limit_bytes=(28 + 3 * len(picks)) << 20),
    )(*scalars, levels, own, *lefts, *used, *begun)


def pack_body(own_a, own_b, up_a, down_a, up_b, down_b, out, total, block):
    for slot, parts in enumerate(((own_a, up_a, down_a), (own_b, up_b, down_b))):
        for k in range(12):
            lanes = slice(k * 128, (k + 1) * 128)
            own, up, down = (part[:, lanes].astype(jnp.float32) for part in parts)
            total[slot * 12 + k] = own + up + down
    for c in range(16):
        tile, offset = divmod(c * 96, 128)
        for slot in range(2):
            pieces = []
            for q in range(4):
                rows = pl.ds(q, 96, stride=4)
                piece = total[slot * 12 + tile, rows, :]
                if offset > 32:
                    piece = jnp.concatenate([piece, total[slot * 12 + tile + 1, rows, :]], 1)
                pieces.append(piece[:, offset : offset + 96])
            value = jnp.concatenate(pieces, 1)
            for k in range(3):
                block[c % 2 * 3 + k, pl.ds(slot, 96, stride=2), :] = value[:, k * 128 : (k + 1) * 128]
        for r in range(8):
            for k in range(3):
                out[r * 16 + c, :, k * 128 : (k + 1) * 128] = block[
                    c % 2 * 3 + k, r * 24 : (r + 1) * 24
                ].astype(out.dtype)


def pack(own_a, own_b, up_a, down_a, up_b, down_b):
    vmem = pl.BlockSpec(memory_space=pltpu.VMEM)
    return pl.pallas_call(
        pack_body,
        out_shape=jax.ShapeDtypeStruct((128, 24, 384), jnp.bfloat16),
        in_specs=[vmem] * 6,
        out_specs=vmem,
        scratch_shapes=[
            pltpu.VMEM((24, 384, 128), jnp.float32),
            pltpu.VMEM((6, 192, 128), jnp.float32),
        ],
        compiler_params=pltpu.CompilerParams(vmem_limit_bytes=20 << 20),
        name="pack",
    )(own_a, own_b, up_a, down_a, up_b, down_b)


def finish_body(blocks, coeff, out, wide):
    step = pl.program_id(0)

    @pl.when(step == 0)
    def _():
        for k in range(3):
            wide[k] = blocks[:, k * 128 : (k + 1) * 128].astype(jnp.float32)

    per_step = out.shape[0] // 4
    for k in range(per_step):
        t = step * per_step + k
        rows = jnp.concatenate(
            [
                jnp.concatenate([wide[k, pl.ds(2 * t + s, 128, stride=24), :] for k in range(3)], 1)
                for s in range(2)
            ],
            0,
        ).astype(jnp.bfloat16)
        result = lax.dot_general(
            rows, coeff[...], (((0,), (1,)), ((), ())),
            preferred_element_type=jnp.float32,
        )
        out[4 * k : 4 * k + 4] = result.reshape(4, 96, 768).astype(out.dtype)


def finish(blocks, coeff):
    rows = 12
    return pl.pallas_call(
        finish_body,
        grid=(48 // rows,),
        out_shape=jax.ShapeDtypeStruct((48, 96, 768), jnp.bfloat16),
        in_specs=[
            pl.BlockSpec((128 * 24, 384), lambda s: (0, 0)),
            pl.BlockSpec((768, 256), lambda s: (0, 0)),
        ],
        out_specs=pl.BlockSpec((rows, 96, 768), lambda s: (s, 0, 0)),
        scratch_shapes=[pltpu.VMEM((3, 128 * 24, 128), jnp.float32)],
        compiler_params=pltpu.CompilerParams(vmem_limit_bytes=20 << 20),
        name="finish",
    )(blocks, coeff)


def split_body(low, high, out_a, out_b, sems):
    copies = [
        pltpu.make_async_copy(low.at[0], out_a, sems.at[0]),
        pltpu.make_async_copy(high.at[1], out_b, sems.at[1]),
    ]
    for copy in copies:
        copy.start()
    for copy in copies:
        copy.wait()


def split(low, high):
    slab = jax.ShapeDtypeStruct(low.shape[1:], low.dtype)
    hbm = pl.BlockSpec(memory_space=pltpu.HBM)
    return pl.pallas_call(
        split_body,
        out_shape=(slab, slab),
        in_specs=[hbm, hbm],
        out_specs=[pl.BlockSpec(memory_space=pltpu.VMEM)] * 2,
        scratch_shapes=[pltpu.SemaphoreType.DMA((2,))],
        name="split",
    )(low, high)


def add(first, *others):
    total = first.astype(jnp.float32)
    for other in others:
        total = total + other.astype(jnp.float32)
    return total.astype(jnp.bfloat16)


def local(b_three, e_occ, e_vir, c_occ, pair_list, pair_live):
    device = lax.axis_index("row") * 16 + lax.axis_index("col")

    right_low = send(b_three, "right", 1)
    right_high = send(b_three, "right", -1)
    own_a, own_b = b_three[0], b_three[1]
    info = jnp.concatenate([pair_list.reshape(1, 32), pair_live.reshape(1, 16)], 1)
    tables = [info] + [send(info, "left", step) for step in (1, -1, 2)]
    near_low_a = send(own_a, "left", 1)
    near_high_b = send(own_b, "left", -1)
    onward_a, onward_b = split(right_low, right_high)
    right_far_a = send(onward_a, "right", 1)
    right_far_b = send(onward_b, "right", -1)
    far_a = send(near_low_a, "left", 1)
    far_b = send(near_high_b, "left", -1)
    own_a, own_b, right_far_a, right_far_b = lax.optimization_barrier(
        (own_a, own_b, right_far_a, right_far_b)
    )
    late_low_b = send(own_b, "left", 1)
    late_high_a = send(own_a, "left", -1)
    rights = ((), (right_low,), (right_high,), (right_far_a, right_far_b))

    def partial(lefts, which, slots, dtype=jnp.bfloat16, picks=(0, 1, 2, 3), begun=()):
        scalars = [device.reshape(1)] + [tables[k] for k in which] + [e_occ]
        return partial_gamma(scalars, e_vir, b_three, lefts, slots, rights, picks, begun, dtype)

    near = (near_low_a, near_high_b)
    begun = partial(near, (1, 2), (0, 1), jnp.float32, (0, 1, 2))
    far = (far_a, far_b)
    ahead = partial(far, (3, 3), (0, 1), jnp.float32, (0, 1, 2))
    far_a, far_b = partial(far, (3, 3), (0, 1), picks=(3,), begun=ahead)
    relay_a = send(far_a, "left", 1)
    relay_b = send(far_b, "left", -1)
    low_b, high_a = partial((late_low_b, late_high_a), (1, 2), (1, 0))
    up_a = send(add(high_a, relay_a), "left", 1)
    down_b = send(add(low_b, relay_b), "left", -1)
    low_a, high_b = partial(near, (1, 2), (0, 1), picks=(3,), begun=begun)
    up_b = send(high_b, "left", 1)
    down_a = send(low_a, "left", -1)
    sum_a, sum_b = partial((b_three, b_three), (0, 0), (0, 1), jnp.float32)

    blocks = pack(sum_a, sum_b, up_a, down_a, up_b, down_b)
    moved = lax.all_to_all(blocks, AXES, split_axis=0, concat_axis=0, tiled=True)
    coeff = c_occ.reshape(-1, 128, 2).transpose(0, 2, 1).reshape(-1, 256)
    return finish(moved.reshape(128 * 24, 384), coeff)


def solution(mesh):
    return jax.shard_map(
        local,
        mesh=mesh,
        in_specs=(
            P(AXES, None, None),
            P(),
            P(),
            P(),
            P(AXES, None, None),
            P(AXES, None),
        ),
        out_specs=P("row", "col", None),
        check_vma=False,
    )
```

```python
import functools

import jax
import jax.numpy as jnp
from jax import lax
from jax.experimental import pallas as pl
from jax.experimental.pallas import tpu as pltpu
from jax.sharding import PartitionSpec as P


AXES = ("row", "col")
SIDE = 4


def shifted(kind, step):
    pairs = []
    for row in range(8):
        for z in range(SIDE):
            for x in range(SIDE):
                along_x = (row % 2 == 0) == (kind == "left")
                to_z, to_x = (z, (x + step) % SIDE) if along_x else ((z + step) % SIDE, x)
                pairs.append((row * 16 + z * SIDE + x, row * 16 + to_z * SIDE + to_x))
    return pairs


def send(value, kind, step):
    return lax.ppermute(value, AXES, shifted(kind, step))


def pair_body(device, table_a, table_b, energies, levels, own, *refs, slots, picks, started):
    count = len(picks)
    lefts, refs = refs[:2], refs[2:]
    if lefts[0].shape == own.shape:
        lefts = (own.at[0], own.at[1])
    rights = []
    for n in picks:
        if n == 3:
            rights += refs[:2]
            refs = refs[2:]
        elif n:
            rights += [refs[0].at[0], refs[0].at[1]]
            refs = refs[1:]
        else:
            rights += [own.at[0], own.at[1]]
    begun, refs = refs[: 2 * started], refs[2 * started :]
    out_a, out_b, left_buf, right_buf, gamma, across, left_sem, right_sem = refs
    outs = (out_a, out_b)
    col = device[0] % 16
    z, x = col // SIDE, col % SIDE
    even = device[0] // 16 % 2 == 0
    columns = [
        jnp.where(even, (z + d) % SIDE * SIDE + x, z * SIDE + (x + d) % SIDE)
        for d in ((0, 3, 1, 2)[n] for n in picks)
    ]

    def entry(m):
        side, n = m // count, m % count
        right = columns[0]
        for k in range(1, count):
            right = jnp.where(n == k, columns[k], right)

        def pick(k):
            return jnp.where(side == 0, table_a[0, k], table_b[0, k])

        first, second, live = pick(right * 2), pick(right * 2 + 1), pick(32 + right)
        wanted = jnp.where(side == 0, slots[0], slots[1])
        return first, second, (live > 0) & (first % 2 == wanted)

    left_copies = [
        pltpu.make_async_copy(left, left_buf.at[s], left_sem.at[s]) for s, left in enumerate(lefts)
    ]
    for copy in left_copies:
        copy.start()
    for m in range(2 * count):
        _, second, taken = entry(m)
        for s in range(2):

            @pl.when(taken & (second % 2 == s))
            def _():
                pltpu.make_async_copy(
                    rights[2 * (m % count) + s], right_buf.at[m], right_sem.at[m]
                ).start()

    for s in range(2):
        gamma[s] = begun[s][...] if started else jnp.zeros(gamma.shape[1:], jnp.float32)
    row = levels[...].reshape(1, levels.shape[-1])
    across[...] = jnp.broadcast_to(row, across.shape).T
    for copy in left_copies:
        copy.wait()

    def step(m, carry):
        first, second, taken = entry(m)

        @pl.when(taken)
        def _():
            pltpu.make_async_copy(rights[0], right_buf.at[m], right_sem.at[m]).wait()
            right = right_buf[m]
            integrals = lax.dot_general(
                left_buf[m // count], right, (((1,), (1,)), ((), ())),
                preferred_element_type=jnp.float32,
            )
            denominator = energies[first] + energies[second] - across[...] - row
            weighted = ((2.0 * integrals - integrals.T) / denominator).astype(jnp.bfloat16)
            gamma[m // count] += jnp.dot(weighted, right, preferred_element_type=jnp.float32)

        return carry

    lax.fori_loop(0, 2 * count, step, 0)
    for s in range(2):
        outs[s][...] = gamma[s].astype(outs[s].dtype)


def partial_gamma(scalars, levels, own, lefts, slots, rights, picks, begun, out_dtype):
    virt, aux = own.shape[1:]
    slab = jax.ShapeDtypeStruct((virt, aux), out_dtype)
    hbm = pl.BlockSpec(memory_space=pltpu.HBM)
    smem = pl.BlockSpec(memory_space=pltpu.SMEM)
    vmem = pl.BlockSpec(memory_space=pltpu.VMEM)
    left_space = hbm if lefts[0] is own else vmem
    used = [slab for n in picks if n for slab in rights[n]]
    return pl.pallas_call(
        functools.partial(pair_body, slots=slots, picks=picks, started=bool(begun)),
        out_shape=(slab, slab),
        in_specs=[smem] * 4
        + [vmem, hbm]
        + [left_space] * 2
        + [hbm] * len(used)
        + [vmem] * len(begun),
        out_specs=(vmem, vmem),
        scratch_shapes=[
            pltpu.VMEM((2, virt, aux), jnp.bfloat16),
            pltpu.VMEM((2 * len(picks), virt, aux), jnp.bfloat16),
            pltpu.VMEM((2, virt, aux), jnp.float32),
            pltpu.VMEM((virt, virt), jnp.float32),
            pltpu.SemaphoreType.DMA((2,)),
            pltpu.SemaphoreType.DMA((2 * len(picks),)),
        ],
        compiler_params=pltpu.CompilerParams(vmem_limit_bytes=(28 + 3 * len(picks)) << 20),
    )(*scalars, levels, own, *lefts, *used, *begun)


def pack_body(own_a, own_b, up_a, down_a, up_b, down_b, out, total, block):
    for slot, parts in enumerate(((own_a, up_a, down_a), (own_b, up_b, down_b))):
        for k in range(12):
            lanes = slice(k * 128, (k + 1) * 128)
            own, up, down = (part[:, lanes].astype(jnp.float32) for part in parts)
            total[slot * 12 + k] = own + up + down
    for c in range(16):
        tile, offset = divmod(c * 96, 128)
        for slot in range(2):
            pieces = []
            for q in range(4):
                rows = pl.ds(q, 96, stride=4)
                piece = total[slot * 12 + tile, rows, :]
                if offset > 32:
                    piece = jnp.concatenate([piece, total[slot * 12 + tile + 1, rows, :]], 1)
                pieces.append(piece[:, offset : offset + 96])
            value = jnp.concatenate(pieces, 1)
            for k in range(3):
                block[c % 2 * 3 + k, pl.ds(slot, 96, stride=2), :] = value[:, k * 128 : (k + 1) * 128]
        for r in range(8):
            for k in range(3):
                out[r * 16 + c, :, k * 128 : (k + 1) * 128] = block[
                    c % 2 * 3 + k, r * 24 : (r + 1) * 24
                ].astype(out.dtype)


def pack(own_a, own_b, up_a, down_a, up_b, down_b):
    vmem = pl.BlockSpec(memory_space=pltpu.VMEM)
    return pl.pallas_call(
        pack_body,
        out_shape=jax.ShapeDtypeStruct((128, 24, 384), jnp.bfloat16),
        in_specs=[vmem] * 6,
        out_specs=vmem,
        scratch_shapes=[
            pltpu.VMEM((24, 384, 128), jnp.float32),
            pltpu.VMEM((6, 192, 128), jnp.float32),
        ],
        compiler_params=pltpu.CompilerParams(vmem_limit_bytes=20 << 20),
        name="pack",
    )(own_a, own_b, up_a, down_a, up_b, down_b)


def finish_body(blocks, coeff, out, wide):
    step = pl.program_id(0)

    @pl.when(step == 0)
    def _():
        for k in range(3):
            wide[k] = blocks[:, k * 128 : (k + 1) * 128].astype(jnp.float32)

    per_step = out.shape[0] // 4
    for k in range(per_step):
        t = step * per_step + k
        rows = jnp.concatenate(
            [
                jnp.concatenate([wide[k, pl.ds(2 * t + s, 128, stride=24), :] for k in range(3)], 1)
                for s in range(2)
            ],
            0,
        ).astype(jnp.bfloat16)
        result = lax.dot_general(
            rows, coeff[...], (((0,), (1,)), ((), ())),
            preferred_element_type=jnp.float32,
        )
        out[4 * k : 4 * k + 4] = result.reshape(4, 96, 768).astype(out.dtype)


def finish(blocks, coeff):
    rows = 12
    return pl.pallas_call(
        finish_body,
        grid=(48 // rows,),
        out_shape=jax.ShapeDtypeStruct((48, 96, 768), jnp.bfloat16),
        in_specs=[
            pl.BlockSpec((128 * 24, 384), lambda s: (0, 0)),
            pl.BlockSpec((768, 256), lambda s: (0, 0)),
        ],
        out_specs=pl.BlockSpec((rows, 96, 768), lambda s: (s, 0, 0)),
        scratch_shapes=[pltpu.VMEM((3, 128 * 24, 128), jnp.float32)],
        compiler_params=pltpu.CompilerParams(vmem_limit_bytes=20 << 20),
        name="finish",
    )(blocks, coeff)


def split_body(low, high, out_a, out_b, sems):
    copies = [
        pltpu.make_async_copy(low.at[0], out_a, sems.at[0]),
        pltpu.make_async_copy(high.at[1], out_b, sems.at[1]),
    ]
    for copy in copies:
        copy.start()
    for copy in copies:
        copy.wait()


def split(low, high):
    slab = jax.ShapeDtypeStruct(low.shape[1:], low.dtype)
    hbm = pl.BlockSpec(memory_space=pltpu.HBM)
    return pl.pallas_call(
        split_body,
        out_shape=(slab, slab),
        in_specs=[hbm, hbm],
        out_specs=[pl.BlockSpec(memory_space=pltpu.VMEM)] * 2,
        scratch_shapes=[pltpu.SemaphoreType.DMA((2,))],
        name="split",
    )(low, high)


def add(first, *others):
    total = first.astype(jnp.float32)
    for other in others:
        total = total + other.astype(jnp.float32)
    return total.astype(jnp.bfloat16)


def local(b_three, e_occ, e_vir, c_occ, pair_list, pair_live):
    device = lax.axis_index("row") * 16 + lax.axis_index("col")

    right_low = send(b_three, "right", 1)
    right_high = send(b_three, "right", -1)
    own_a, own_b = b_three[0], b_three[1]
    info = jnp.concatenate([pair_list.reshape(1, 32), pair_live.reshape(1, 16)], 1)
    tables = [info] + [send(info, "left", step) for step in (1, -1, 2)]
    near_low_a = send(own_a, "left", 1)
    near_high_b = send(own_b, "left", -1)
    onward_a, onward_b = split(right_low, right_high)
    right_far_a = send(onward_a, "right", 1)
    right_far_b = send(onward_b, "right", -1)
    far_a = send(near_low_a, "left", 1)
    far_b = send(near_high_b, "left", -1)
    own_a, own_b, right_far_a, right_far_b, far_a, far_b = lax.optimization_barrier(
        (own_a, own_b, right_far_a, right_far_b, far_a, far_b)
    )
    late_low_b = send(own_b, "left", 1)
    late_high_a = send(own_a, "left", -1)
    rights = ((), (right_low,), (right_high,), (right_far_a, right_far_b))

    def partial(lefts, which, slots, dtype=jnp.bfloat16, picks=(0, 1, 2, 3), begun=()):
        scalars = [device.reshape(1)] + [tables[k] for k in which] + [e_occ]
        return partial_gamma(scalars, e_vir, b_three, lefts, slots, rights, picks, begun, dtype)

    near = (near_low_a, near_high_b)
    begun = partial(near, (1, 2), (0, 1), jnp.float32, (0, 1, 2))
    far_a, far_b = partial((far_a, far_b), (3, 3), (0, 1))
    relay_a = send(far_a, "left", 1)
    relay_b = send(far_b, "left", -1)
    low_b, high_a = partial((late_low_b, late_high_a), (1, 2), (1, 0))
    up_a = send(add(high_a, relay_a), "left", 1)
    down_b = send(add(low_b, relay_b), "left", -1)
    low_a, high_b = partial(near, (1, 2), (0, 1), picks=(3,), begun=begun)
    up_b = send(high_b, "left", 1)
    down_a = send(low_a, "left", -1)
    sum_a, sum_b = partial((b_three, b_three), (0, 0), (0, 1), jnp.float32)

    blocks = pack(sum_a, sum_b, up_a, down_a, up_b, down_b)
    moved = lax.all_to_all(blocks, AXES, split_axis=0, concat_axis=0, tiled=True)
    coeff = c_occ.reshape(-1, 128, 2).transpose(0, 2, 1).reshape(-1, 256)
    return finish(moved.reshape(128 * 24, 384), coeff)


def solution(mesh):
    return jax.shard_map(
        local,
        mesh=mesh,
        in_specs=(
            P(AXES, None, None),
            P(),
            P(),
            P(),
            P(AXES, None, None),
            P(AXES, None),
        ),
        out_specs=P("row", "col", None),
        check_vma=False,
    )
```
